32 devices in a mesh: leaf: 8 (over z, x), vec: 4 (over y, core).
Axes of the slice: x: 2, y: 2, z: 4, core: 2. Of those that a mesh axis runs over, the one named last changes fastest.
Arguments:
- panels: float32 [32, 65536], P('vec', 'leaf'), may hold values from -6 to 6
- near_tiles: float32 [512, 4, 128, 128], P('leaf', None, 'vec'), may hold values from -0.25 to 0.25
- near_cols: int32 [512, 4], P('leaf'), may hold values from 0 to 511, as said below
- leaf_order: int32 [512, 128], P('leaf'), may hold values from 0 to 127, each once within a row
- leaf_basis: float32 [512, 64, 128], P('leaf'), may hold values from -0.5 to 0.5
- local_mats: float32 [8, 63, 64, 128], P('leaf'), may hold values from -0.75 to 0.75
- local_flags: int32 [8, 63], P('leaf'), may hold values 0 or 1
- cross_coupling: float32 [6, 64, 64], replicated, may hold values from -0.75 to 0.75
- cross_transfer: float32 [4, 64, 64], replicated, may hold values from -0.75 to 0.75
- cross_flags: int32 [6], replicated, may hold values 0 or 1
Outputs:
- product: float32 [32, 65536], P('vec', 'leaf')
The draws below stay inside these ranges and needn't reach their ends.
Inputs may be any that keep to these rules, and one draw needn't show every extreme that they name: `near_cols`: every entry of row i names a leaf within 8 leaves of leaf i. `leaf_order`: each row is a permutation of 0 to 127.
All inputs are finite; a program needn't handle non-finite values. No bound on the sum of `local_flags` on one device may be relied on, other than what follows from the above.
Results may differ from the reference program's by a relative error of at most 0.00022.
Values sent between devices are 32-bit elements; how exact they have to be, the bound alone decides.
A program may use at most 64 MiB of HBM per device.

```python
import math
import jax
import jax.numpy as jnp
from jax import lax

M = 128
K = 64
R = 32
NEAR = 4
W = 8
LEAF_DEV = 64
LEAVES = 512
PANELS = 65536
LOCAL_DEPTH = 6
LEAF_DEPTH = 3
N_LEAF = 8


def draw_near_cols(key, part):
    row_ids = jnp.arange(LEAVES, dtype=jnp.int32)[:, None]
    offsets = jax.random.randint(key, (LEAVES, NEAR), -W, W + 1, dtype=jnp.int32)
    offsets = offsets.at[0, 0].set(W).at[LEAVES - 1, 0].set(-W)
    return jnp.clip(row_ids + offsets, 0, LEAVES - 1).astype(jnp.int32)


def touch_ends(values, key, smallest, largest):
    spot = [jax.random.randint(jax.random.fold_in(key, axis), (), 0, length) for axis, length in enumerate(values.shape)]
    widest = values.shape.index(max(values.shape))
    next_to = spot[:widest] + [(spot[widest] + 1) % values.shape[widest]] + spot[widest + 1:]
    return values.at[tuple(spot)].set(smallest).at[tuple(next_to)].set(largest)


def steps_of(stream_key, shape, shards, low, top_value):
    def one(axis_at, blocks):
        draws = jax.random.uniform(jax.random.fold_in(jax.random.fold_in(stream_key, 6), axis_at), (blocks,), jnp.float32, low / len(shards), top_value / len(shards))
        return jnp.repeat(jnp.exp(draws), shape[axis_at] // blocks).reshape((-1,) + (1,) * (len(shape) - axis_at - 1))

    factor_of = one(*shards[0])
    for cut in shards[1:]:
        factor_of = factor_of * one(*cut)
    return factor_of


def scatter_about(stream_key, extent, scale, limit, split=(), kind=jnp.bfloat16):
    values = jax.random.normal(stream_key, extent, jnp.float32) * scale
    if len(split) > 0:
        values = steps_of(stream_key, extent, split, -0.22, 0.18) * values
    return jnp.clip(values, min=-limit, max=limit).astype(kind)


def setup_inputs(seed: int = 0) -> dict:
    splits = jax.random.split(jax.random.key(seed), 11)
    panels = scatter_about(splits[0], (R, PANELS), 1.0, 6.0, ((0, 4), (1, 8)), jnp.float32)
    near_tiles = scatter_about(splits[1], (LEAVES, NEAR, M, M), (NEAR * M) ** -0.5, 0.25, ((0, 8), (2, 4)), jnp.float32)
    near_cols = draw_near_cols(jax.random.fold_in(splits[10], 71), 0)
    leaf_order = jax.vmap(lambda own: jax.random.permutation(own, M))(jax.random.split(splits[3], LEAVES)).reshape((LEAVES, M)).astype(jnp.int32)
    leaf_basis = scatter_about(splits[4], (LEAVES, K, M), M ** -0.5, 0.5, ((0, 8),), jnp.float32)
    local_mats = scatter_about(splits[5], (LEAVES // LEAF_DEV, LEAF_DEV - 1, K, 2 * K), K ** -0.5, 0.75, ((0, 8),), jnp.float32)
    local_flags = touch_ends((jax.random.randint(splits[6], (LEAVES // LEAF_DEV, LEAF_DEV - 1), 0, 4) < 3).astype(jnp.int32), jax.random.fold_in(splits[6], 1), 0, 1)
    cross_coupling = scatter_about(splits[7], (LEAVES // LEAF_DEV - 2, K, K), K ** -0.5, 0.75, (), jnp.float32)
    cross_transfer = scatter_about(splits[8], (LEAVES // LEAF_DEV - 4, K, K), K ** -0.5, 0.75, (), jnp.float32)
    cross_flags = touch_ends((jax.random.randint(splits[9], (LEAVES // LEAF_DEV - 2,), 0, 4) < 3).astype(jnp.int32), jax.random.fold_in(splits[9], 1), 0, 1)
    return dict(panels=panels, near_tiles=near_tiles, near_cols=near_cols, leaf_order=leaf_order, leaf_basis=leaf_basis, local_mats=local_mats, local_flags=local_flags, cross_coupling=cross_coupling, cross_transfer=cross_transfer, cross_flags=cross_flags)


precise = lax.Precision.HIGHEST
root_half = 1.0 / math.sqrt(2.0)

def swap_pairs(nodes):
    halves = nodes.reshape((nodes.shape[0] // 2, 2) + nodes.shape[1:])
    return halves[:, ::-1].reshape(nodes.shape)

def level_blocks(tree_level, local_mats, local_flags, cross_coupling, cross_transfer, cross_flags):
    if tree_level <= LOCAL_DEPTH:
        per_device = LEAF_DEV // 2 ** tree_level
        first_node = LEAF_DEV - LEAF_DEV // 2 ** (tree_level - 1)
        blocks = local_mats[:, first_node:first_node + per_device].reshape(N_LEAF * per_device, K, 2 * K)
        admits = local_flags[:, first_node:first_node + per_device].reshape(N_LEAF * per_device)
        return (blocks[:, :, :K], blocks[:, :, K:], admits)
    cross_level = tree_level - LOCAL_DEPTH
    node_count = N_LEAF // 2 ** cross_level
    first_node = N_LEAF - N_LEAF // 2 ** (cross_level - 1)
    couplings = cross_coupling[first_node:first_node + node_count]
    admits = cross_flags[first_node:first_node + node_count]
    if cross_level <= LEAF_DEPTH - 2:
        return (couplings, cross_transfer[first_node:first_node + node_count], admits)
    return (couplings, couplings, admits)

def reference(panels, near_tiles, near_cols, leaf_order, leaf_basis, local_mats, local_flags, cross_coupling, cross_transfer, cross_flags):
    rhs_count = panels.shape[0]
    order_full = jnp.broadcast_to(leaf_order[None], (rhs_count, LEAVES, M))
    ordered = jnp.take_along_axis(panels.reshape(rhs_count, LEAVES, M), order_full, axis=2)

    def near_block(block_pair):
        tile_block, columns = block_pair
        sources = ordered[:, columns]
        return jnp.einsum('lnqp,slnp->slq', tile_block, sources, precision=precise)
    blocks = lax.map(near_block, (near_tiles.reshape(N_LEAF, LEAF_DEV, NEAR, M, M), near_cols.reshape(N_LEAF, LEAF_DEV, NEAR)))
    near_field = jnp.transpose(blocks, (1, 0, 2, 3)).reshape(rhs_count, LEAVES, M)
    leaf_skel = jnp.einsum('lkp,slp->lsk', leaf_basis, ordered, precision=precise)
    skeleton = leaf_skel.reshape(LEAVES // 2, 2, rhs_count, K).sum(axis=1) * root_half
    top_level = LOCAL_DEPTH + LEAF_DEPTH - 1
    coupled = []
    transfers = []
    for tree_level in range(1, top_level + 1):
        couplings, transfer, admits = level_blocks(tree_level, local_mats, local_flags, cross_coupling, cross_transfer, cross_flags)
        term = jnp.einsum('jkm,jsm->jsk', couplings, swap_pairs(skeleton), precision=precise)
        coupled.append(admits.astype(jnp.float32)[:, None, None] * term)
        transfers.append(transfer)
        if tree_level < top_level:
            lifted = jnp.einsum('jsk,jkm->jsm', skeleton, transfer, precision=precise)
            skeleton = lifted.reshape(lifted.shape[0] // 2, 2, rhs_count, K).sum(axis=1) * root_half
    downward = coupled[top_level - 1]
    for tree_level in range(top_level - 1, 0, -1):
        spread = jnp.repeat(downward, 2, axis=0)
        downward = coupled[tree_level - 1] + jnp.einsum('jkm,jsm->jsk', transfers[tree_level - 1], spread, precision=precise)
    far_field = jnp.einsum('lkp,lsk->slp', leaf_basis, jnp.repeat(downward, 2, axis=0), precision=precise)
    combined = near_field + far_field
    inverse = jnp.argsort(leaf_order, axis=1).astype(jnp.int32)
    restored = jnp.take_along_axis(combined, jnp.broadcast_to(inverse[None], (rhs_count, LEAVES, M)), axis=2)
    return restored.reshape(rhs_count, PANELS)
```

```python
import functools
import math

import jax
import jax.numpy as jnp
from jax import lax
from jax.experimental import pallas as pl
from jax.experimental.pallas import tpu as pltpu
from jax.sharding import PartitionSpec as P

W = 8
f32 = jnp.float32
bf16 = jnp.bfloat16
root_half = 1.0 / math.sqrt(2.0)
MESH = pl.DeviceIdType.MESH
NN = (((1,), (0,)), ((), ()))
NT = (((1,), (1,)), ((), ()))


def halves(x):
    high = x.astype(bf16).astype(f32)
    return high, x - high


def stacked(x):
    return jnp.concatenate(halves(x), axis=0).astype(bf16)


def dot_split(x, w, dims):
    rows = x.shape[0]
    lhs = stacked(x)
    high = w.astype(bf16)
    low = (w - high.astype(f32)).astype(bf16)
    r = lax.dot_general(lhs, high, dims, preferred_element_type=f32) + lax.dot_general(
        lhs, low, dims, preferred_element_type=f32
    )
    return r[:rows] + r[rows:]


def hot_of(order_row):
    size = order_row.shape[1]
    rows = lax.broadcasted_iota(jnp.int32, (size, size), 0)
    return jnp.where(rows == order_row, 1.0, 0.0).astype(bf16)


def order_kernel(panels_ref, order_ref, out_ref):
    leaves, size = order_ref.shape
    span = 8

    def body(i, carry):
        for u in range(span):
            leaf = i * span + u
            hot = hot_of(order_ref[pl.ds(leaf, 1), :])
            x = stacked(panels_ref[:, pl.ds(pl.multiple_of(leaf * size, size), size)])
            r = lax.dot_general(x, hot, NN, preferred_element_type=f32)
            rows = panels_ref.shape[0]
            out_ref[leaf] = r[:rows] + r[rows:]
        return carry

    lax.fori_loop(0, leaves // span, body, 0)


def restore_kernel(far_ref, near_ref, order_ref, out_ref):
    leaves, size = order_ref.shape
    n_vec = near_ref.shape[0]
    piece = size // n_vec
    rows = out_ref.shape[0]
    block = lax.broadcasted_iota(jnp.int32, (rows, size), 1) // piece

    def body(g, carry):
        parts = [near_ref[v, g] for v in range(n_vec)]
        for u in range(n_vec):
            leaf = g * n_vec + u
            near = parts[0] if u == 0 else pltpu.roll(parts[0], (size - u * piece), 1)
            for v in range(1, n_vec):
                shift = ((v - u) * piece) % size
                moved = parts[v] if shift == 0 else pltpu.roll(parts[v], shift, 1)
                near = jnp.where(block == v, moved, near)
            combined = near + far_ref[leaf]
            hot = hot_of(order_ref[pl.ds(leaf, 1), :])
            r = lax.dot_general(stacked(combined), hot, NT, preferred_element_type=f32)
            out_ref[:, pl.ds(pl.multiple_of(leaf * size, size), size)] = r[:rows] + r[rows:]
        return carry

    lax.fori_loop(0, leaves // n_vec, body, 0)


def main_kernel(
    n_leaf,
    n_vec,
    own_ref,
    cols_ref,
    flags_ref,
    cross_flags_ref,
    cross_c_ref,
    cross_e_ref,
    tiles_hbm,
    basis_hbm,
    mats_hbm,
    far_ref,
    near_ref,
    tiles,
    basis,
    mats,
    ext,
    xs,
    hp,
    zp,
    pay,
    hx,
    nout,
    load_sem,
    gs_send,
    gs_recv,
    halo_send,
    halo_recv,
    pay_send,
    pay_recv,
    near_send,
    near_recv,
):
    leaves = own_ref.shape[0]
    rank = 64
    li = lax.axis_index("leaf")
    vi = lax.axis_index("vec")
    load_b = pltpu.make_async_copy(basis_hbm, basis, load_sem.at[0])
    load_m = pltpu.make_async_copy(mats_hbm, mats, load_sem.at[1])
    load_t = pltpu.make_async_copy(tiles_hbm, tiles, load_sem.at[2])
    load_o = pltpu.make_async_copy(own_ref, ext.at[vi, pl.ds(W, leaves)], load_sem.at[3])
    load_b.start()
    load_m.start()
    load_t.start()
    load_o.start()

    right = lax.rem(li + 1, n_leaf)
    left = lax.rem(li + n_leaf - 1, n_leaf)
    barrier = pltpu.get_barrier_semaphore()
    greeted = 0
    for d in range(1, n_vec):
        pl.semaphore_signal(
            barrier, inc=1, device_id=(li, lax.rem(vi + d, n_vec)), device_id_type=MESH
        )
        greeted += 1
    for side in (left, right):
        for u in range(n_vec):
            pl.semaphore_signal(
                barrier, inc=1, device_id=(side, lax.rem(vi + u, n_vec)), device_id_type=MESH
            )
            greeted += 1
    for d in range(2, n_leaf - 1):
        pl.semaphore_signal(
            barrier, inc=1, device_id=(lax.rem(li + d, n_leaf), vi), device_id_type=MESH
        )
        greeted += 1
    pl.semaphore_wait(barrier, greeted)

    def gather_copy(d):
        return pltpu.make_async_remote_copy(
            src_ref=own_ref,
            dst_ref=ext.at[vi, pl.ds(W, leaves)],
            send_sem=gs_send.at[d],
            recv_sem=gs_recv.at[n_vec - d],
            device_id=(li, lax.rem(vi + d, n_vec)),
            device_id_type=MESH,
        )

    def halo_copy(side, d):
        start = leaves - W if side == 0 else 0
        to = 0 if side == 0 else leaves + W
        return pltpu.make_async_remote_copy(
            src_ref=own_ref.at[pl.ds(start, W)],
            dst_ref=ext.at[vi, pl.ds(to, W)],
            send_sem=halo_send.at[side, d],
            recv_sem=halo_recv.at[side, (n_vec - d) % n_vec],
            device_id=(right if side == 0 else left, lax.rem(vi + d, n_vec)),
            device_id_type=MESH,
        )

    gathers = [gather_copy(d) for d in range(1, n_vec)]
    halos = [halo_copy(side, d) for side in range(2) for d in range(n_vec)]
    for c in halos + gathers:
        c.start()

    lane = lax.broadcasted_iota(jnp.int32, (8, 2 * rank), 1)
    low = lane < rank

    def swap(x):
        return pltpu.roll(x, rank, 1)

    load_b.wait()

    def skel_body(i, carry):
        for w in range(2):
            t = i * 2 + w
            sums = []
            for u in range(2):
                pair = t * 2 + u
                x = own_ref[pl.ds(pair * 2, 2)].reshape(16, 128)
                wt = basis[pl.ds(pl.multiple_of(pair * 128, 128), 128), :]
                r = dot_split(x, wt, NT)
                sums.append((r[:8], r[8:]))
            even = sums[0][0] + swap(sums[0][1])
            odd = swap(sums[1][0]) + sums[1][1]
            hp[t] = jnp.where(low, even, odd) * root_half
        return carry

    lax.fori_loop(0, leaves // 8, skel_body, 0)
    load_m.wait()

    def mat_pair(q):
        return mats[pl.ds(pl.multiple_of(q * 128, 128), 128), :]

    def up(off, nxt, t):
        r0 = dot_split(hp[off + 2 * t], mat_pair(off + 2 * t), NN)
        r1 = dot_split(hp[off + 2 * t + 1], mat_pair(off + 2 * t + 1), NN)
        hp[nxt + t] = jnp.where(low, swap(r0), r1) * root_half

    pairs = leaves // 4
    offs = []
    off = 0
    while pairs >= 1:
        offs.append((off, pairs))
        off += pairs
        pairs //= 2
    for (a, count), (b, half) in zip(offs[:-1], offs[1:]):
        if half > 4:
            def up_body(i, carry, a=a, b=b):
                for w in range(4):
                    up(a, b, i * 4 + w)
                return carry

            lax.fori_loop(0, half // 4, up_body, 0)
        else:
            for t in range(half):
                up(a, b, t)
    last = offs[-1][0]
    r = dot_split(hp[last], mat_pair(last), NN)
    skel = swap(r) * root_half
    top = mats[pl.ds((last + 1) * 128, rank), :]
    lift = dot_split(skel[:, :rank], top, NN)
    pay[li] = jnp.where(low, skel, lift)

    def pay_copy(d):
        return pltpu.make_async_remote_copy(
            src_ref=pay.at[li],
            dst_ref=pay.at[li],
            send_sem=pay_send.at[d],
            recv_sem=pay_recv.at[n_leaf - d],
            device_id=(lax.rem(li + d, n_leaf), vi),
            device_id_type=MESH,
        )

    pays = [pay_copy(d) for d in range(1, n_leaf)]
    for c in pays:
        c.start()

    load_o.wait()
    load_t.wait()
    for c in halos + gathers:
        c.wait_recv()
    for c in halos + gathers:
        c.wait_send()

    def split_body(i, carry):
        for w in range(4):
            e = i * 4 + w
            xs[e] = stacked(ext[:, e].reshape(n_vec * 8, 128))
        return carry

    lax.fori_loop(0, (leaves + 2 * W) // 4, split_body, 0)
    base = li * leaves - W
    slots = tiles.shape[1]
    piece = tiles.shape[2]

    def place(leaf, n):
        return jnp.clip(cols_ref[leaf, n] - base, 0, leaves + 2 * W - 1)

    def near_body(g, carry):
        outs = []
        for w in range(n_vec):
            leaf = g * n_vec + w
            x = jnp.concatenate([xs[place(leaf, n)] for n in range(slots)], axis=1)
            t = jnp.concatenate([stacked(tiles[leaf, n]) for n in range(slots)], axis=1)
            r = lax.dot_general(x, t, NT, preferred_element_type=f32)
            half = r.shape[0] // 2
            r = r[:half] + r[half:]
            outs.append(r[:, :piece] + r[:, piece:])
        nout[:, g] = jnp.concatenate(outs, axis=1).reshape(n_vec, 8, n_vec * piece)
        return carry

    lax.fori_loop(0, leaves // n_vec, near_body, 0)

    def near_copy(d):
        u = lax.rem(vi + d, n_vec)
        return pltpu.make_async_remote_copy(
            src_ref=nout.at[u],
            dst_ref=near_ref.at[vi],
            send_sem=near_send.at[d],
            recv_sem=near_recv.at[n_vec - d],
            device_id=(li, u),
            device_id_type=MESH,
        )

    nears = [near_copy(d) for d in range(1, n_vec)]
    for c in nears:
        c.start()
    keep = pltpu.make_async_copy(nout.at[vi], near_ref.at[vi], near_send.at[0])
    keep.start()

    for c in pays:
        c.wait_recv()
    for c in pays:
        c.wait_send()

    depth = n_leaf.bit_length() - 1

    def cross_at(c):
        return n_leaf - (n_leaf >> (c - 1))

    lifts = [pay[j] for j in range(n_leaf)]
    at = 0
    starts = {}
    for c in range(1, depth):
        nodes = [
            (lifts[2 * j] + lifts[2 * j + 1]) * root_half for j in range(len(lifts) // 2)
        ]
        nodes = [swap(x) if c == 1 else x for x in nodes]
        starts[c] = at
        for j, x in enumerate(nodes):
            hx[at + j] = x
        at += len(nodes)
        if c < depth - 1:
            lifts = []
            for j, x in enumerate(nodes):
                y = dot_split(x[:, :rank], cross_e_ref[cross_at(c) + j], NN)
                lifts.append(jnp.concatenate([y, y], axis=1))
    z = None
    for c in range(depth - 1, 0, -1):
        node = li >> c
        sibling = node + 1 - 2 * lax.rem(node, 2)
        spot = cross_at(c) + node
        a = cross_flags_ref[spot].astype(f32)
        g = dot_split(a * hx[starts[c] + sibling][:, :rank], cross_c_ref[spot], NT)
        z = g if z is None else g + dot_split(z, cross_e_ref[spot], NT)
    sibling = li + 1 - 2 * lax.rem(li, 2)
    a = flags_ref[0, 2 * (last + 1)].astype(f32)
    x = jnp.where(low, a * pay[sibling], jnp.concatenate([z, z], axis=1))
    z = dot_split(x, top, NT)
    z = jnp.concatenate([z, z], axis=1)

    def down(q, parent):
        h = hp[q]
        a0 = flags_ref[0, 2 * q].astype(f32)
        a1 = flags_ref[0, 2 * q + 1].astype(f32)
        x0 = jnp.where(low, a0 * swap(h), parent)
        x1 = jnp.where(low, a1 * h, parent)
        r = dot_split(jnp.concatenate([x0, x1], axis=0), mat_pair(q), NT)
        zp[q] = jnp.where(low, r[:8], r[8:])

    down(last, z)
    for (a, count), (b, half) in list(zip(offs[:-1], offs[1:]))[::-1]:
        def down_one(t, a=a, b=b):
            p = zp[b + t]
            down(a + 2 * t, swap(p))
            down(a + 2 * t + 1, p)

        if half > 4:
            def down_body(i, carry, down_one=down_one):
                for w in range(4):
                    down_one(i * 4 + w)
                return carry

            lax.fori_loop(0, half // 4, down_body, 0)
        else:
            for t in range(half):
                down_one(t)

    def far_body(i, carry):
        for w in range(2):
            t = i * 2 + w
            p = zp[t]
            s = swap(p)
            zero = jnp.zeros_like(p)
            for u in range(2):
                pair = 2 * t + u
                first, second = (p, s) if u == 0 else (s, p)
                x = jnp.concatenate(
                    [jnp.where(low, first, zero), jnp.where(low, zero, second)], axis=0
                )
                wt = basis[pl.ds(pl.multiple_of(pair * 128, 128), 128), :]
                r = dot_split(x, wt, NN)
                far_ref[2 * pair] = r[:8]
                far_ref[2 * pair + 1] = r[8:]
        return carry

    lax.fori_loop(0, leaves // 8, far_body, 0)
    keep.wait()
    for c in nears:
        c.wait_recv()
    for c in nears:
        c.wait_send()


def local(
    panels,
    near_tiles,
    near_cols,
    leaf_order,
    leaf_basis,
    local_mats,
    local_flags,
    cross_coupling,
    cross_transfer,
    cross_flags,
):
    rows = panels.shape[0]
    leaves, rank, size = leaf_basis.shape
    n_leaf = lax.axis_size("leaf")
    n_vec = lax.axis_size("vec")
    vmem = pl.BlockSpec(memory_space=pltpu.VMEM)
    smem = pl.BlockSpec(memory_space=pltpu.SMEM)
    hbm = pl.BlockSpec(memory_space=pl.ANY)
    ordered = pl.pallas_call(
        order_kernel,
        out_shape=jax.ShapeDtypeStruct((leaves, rows, size), f32),
        in_specs=[vmem, vmem],
        out_specs=vmem,
        name="order",
    )(panels, leaf_order)
    basis2 = leaf_basis.reshape(leaves * rank, size)
    mats2 = local_mats.reshape(local_mats.shape[1] * rank, 2 * rank)
    groups = leaves // n_vec
    dma = pltpu.SemaphoreType.DMA
    far, near = pl.pallas_call(
        functools.partial(main_kernel, n_leaf, n_vec),
        out_shape=(
            jax.ShapeDtypeStruct((leaves, rows, size), f32),
            jax.ShapeDtypeStruct((n_vec, groups, rows, size), f32),
        ),
        in_specs=[vmem, smem, smem, smem, vmem, vmem, hbm, hbm, hbm],
        out_specs=(vmem, vmem),
        scratch_shapes=[
            pltpu.VMEM(near_tiles.shape, f32),
            pltpu.VMEM(basis2.shape, f32),
            pltpu.VMEM(mats2.shape, f32),
            pltpu.VMEM((n_vec, leaves + 2 * W, rows, size), f32),
            pltpu.VMEM((leaves + 2 * W, 2 * n_vec * rows, size), bf16),
            pltpu.VMEM((leaves // 2, rows, size), f32),
            pltpu.VMEM((leaves // 2, rows, size), f32),
            pltpu.VMEM((n_leaf, rows, 2 * rank), f32),
            pltpu.VMEM((n_leaf, rows, 2 * rank), f32),
            pltpu.VMEM((n_vec, groups, rows, size), f32),
            dma((4,)),
            dma((n_vec,)),
            dma((n_vec,)),
            dma((2, n_vec)),
            dma((2, n_vec)),
            dma((n_leaf,)),
            dma((n_leaf,)),
            dma((n_vec,)),
            dma((n_vec,)),
        ],
        compiler_params=pltpu.CompilerParams(
            collective_id=0, has_side_effects=True, vmem_limit_bytes=40 * 1024 * 1024
        ),
        name="tree",
    )(
        ordered,
        near_cols,
        local_flags,
        cross_flags,
        cross_coupling,
        cross_transfer,
        near_tiles,
        basis2,
        mats2,
    )
    return pl.pallas_call(
        restore_kernel,
        out_shape=jax.ShapeDtypeStruct(panels.shape, f32),
        in_specs=[vmem, vmem, vmem],
        out_specs=vmem,
        name="restore",
    )(far, near, leaf_order)


def solution(mesh):
    return jax.shard_map(
        local,
        mesh=mesh,
        in_specs=(
            P("vec", "leaf"),
            P("leaf", None, "vec", None),
            P("leaf", None),
            P("leaf", None),
            P("leaf", None, None),
            P("leaf", None, None, None),
            P("leaf", None),
            P(),
            P(),
            P(),
        ),
        out_specs=P("vec", "leaf"),
        check_vma=False,
    )
```

```python
import functools
import math

import jax
import jax.numpy as jnp
from jax import lax
from jax.experimental import pallas as pl
from jax.experimental.pallas import tpu as pltpu
from jax.sharding import PartitionSpec as P

W = 8
f32 = jnp.float32
bf16 = jnp.bfloat16
root_half = 1.0 / math.sqrt(2.0)
MESH = pl.DeviceIdType.MESH
NN = (((1,), (0,)), ((), ()))
NT = (((1,), (1,)), ((), ()))


def halves(x):
    high = x.astype(bf16).astype(f32)
    return high, x - high


def stacked(x):
    return jnp.concatenate(halves(x), axis=0).astype(bf16)


def dot_split(x, w, dims):
    rows = x.shape[0]
    lhs = stacked(x)
    high = w.astype(bf16)
    low = (w - high.astype(f32)).astype(bf16)
    r = lax.dot_general(lhs, high, dims, preferred_element_type=f32) + lax.dot_general(
        lhs, low, dims, preferred_element_type=f32
    )
    return r[:rows] + r[rows:]


def hot_of(order_row):
    size = order_row.shape[1]
    rows = lax.broadcasted_iota(jnp.int32, (size, size), 0)
    return jnp.where(rows == order_row, 1.0, 0.0).astype(bf16)


def order_kernel(panels_ref, order_ref, out_ref):
    leaves, size = order_ref.shape
    span = 8

    def body(i, carry):
        for u in range(span):
            leaf = i * span + u
            x = panels_ref[:, pl.ds(pl.multiple_of(leaf * size, size), size)]
            spots = jnp.broadcast_to(order_ref[pl.ds(leaf, 1), :], x.shape)
            out_ref[leaf] = jnp.take_along_axis(x, spots, axis=1)
        return carry

    lax.fori_loop(0, leaves // span, body, 0)


def restore_kernel(far_ref, near_ref, inverse_ref, out_ref):
    leaves, _, size = far_ref.shape
    n_vec = near_ref.shape[0]
    piece = size // n_vec
    rows = out_ref.shape[0]
    block = lax.broadcasted_iota(jnp.int32, (rows, size), 1) // piece

    def body(g, carry):
        parts = [near_ref[v, g] for v in range(n_vec)]
        for u in range(n_vec):
            leaf = g * n_vec + u
            near = parts[0] if u == 0 else pltpu.roll(parts[0], (size - u * piece), 1)
            for v in range(1, n_vec):
                shift = ((v - u) * piece) % size
                moved = parts[v] if shift == 0 else pltpu.roll(parts[v], shift, 1)
                near = jnp.where(block == v, moved, near)
            combined = near + far_ref[leaf]
            spots = inverse_ref[leaf].astype(jnp.int32)
            out_ref[:, pl.ds(pl.multiple_of(leaf * size, size), size)] = jnp.take_along_axis(
                combined, spots, axis=1
            )
        return carry

    lax.fori_loop(0, leaves // n_vec, body, 0)


def main_kernel(
    n_leaf,
    n_vec,
    own_ref,
    order_ref,
    cols_hbm,
    flags_hbm,
    cross_flags_hbm,
    cross_c_hbm,
    cross_e_hbm,
    tiles_hbm,
    basis_hbm,
    mats_hbm,
    far_ref,
    near_ref,
    inverse_ref,
    cols_ref,
    flags_ref,
    cross_flags_ref,
    cross_c_ref,
    cross_e_ref,
    tiles,
    basis,
    mats,
    ext,
    xs,
    hp,
    zp,
    pay,
    hx,
    nout,
    load_sem,
    gs_send,
    gs_recv,
    halo_send,
    halo_recv,
    pay_send,
    pay_recv,
    near_send,
    near_recv,
):
    leaves = own_ref.shape[0]
    rank = 64
    li = lax.axis_index("leaf")
    vi = lax.axis_index("vec")
    load_b = pltpu.make_async_copy(basis_hbm, basis, load_sem.at[0])
    load_m = pltpu.make_async_copy(mats_hbm, mats, load_sem.at[1])
    load_t = pltpu.make_async_copy(tiles_hbm, tiles, load_sem.at[2])
    load_o = pltpu.make_async_copy(own_ref, ext.at[vi, pl.ds(W, leaves)], load_sem.at[3])
    load_b.start()
    load_m.start()
    load_t.start()
    load_o.start()
    small = [
        pltpu.make_async_copy(src, dst, load_sem.at[4 + i])
        for i, (src, dst) in enumerate(
            [
                (cols_hbm, cols_ref),
                (flags_hbm, flags_ref),
                (cross_flags_hbm, cross_flags_ref),
                (cross_c_hbm, cross_c_ref),
                (cross_e_hbm, cross_e_ref),
            ]
        )
    ]
    for c in small:
        c.start()

    right = lax.rem(li + 1, n_leaf)
    left = lax.rem(li + n_leaf - 1, n_leaf)
    barrier = pltpu.get_barrier_semaphore()
    greeted = 0
    for d in range(1, n_vec):
        pl.semaphore_signal(
            barrier, inc=1, device_id=(li, lax.rem(vi + d, n_vec)), device_id_type=MESH
        )
        greeted += 1
    for side in (left, right):
        for u in range(n_vec):
            pl.semaphore_signal(
                barrier, inc=1, device_id=(side, lax.rem(vi + u, n_vec)), device_id_type=MESH
            )
            greeted += 1
    for d in range(2, n_leaf - 1):
        pl.semaphore_signal(
            barrier, inc=1, device_id=(lax.rem(li + d, n_leaf), vi), device_id_type=MESH
        )
        greeted += 1
    pl.semaphore_wait(barrier, greeted)

    beside = vi + 1 - 2 * lax.rem(vi, 2)
    across = lax.rem(vi + 2, n_vec)

    def gather_copy(kind):
        block = ext.at[across if kind == 2 else vi, pl.ds(W, leaves)]
        return pltpu.make_async_remote_copy(
            src_ref=block if kind == 2 else own_ref,
            dst_ref=block,
            send_sem=gs_send.at[kind],
            recv_sem=gs_recv.at[kind],
            device_id=(li, across if kind == 0 else beside),
            device_id_type=MESH,
        )

    def halo_copy(side, d):
        start = leaves - W if side == 0 else 0
        to = 0 if side == 0 else leaves + W
        return pltpu.make_async_remote_copy(
            src_ref=own_ref.at[pl.ds(start, W)],
            dst_ref=ext.at[vi, pl.ds(to, W)],
            send_sem=halo_send.at[side, d],
            recv_sem=halo_recv.at[side, (n_vec - d) % n_vec],
            device_id=(right if side == 0 else left, lax.rem(vi + d, n_vec)),
            device_id_type=MESH,
        )

    assert n_vec == 4
    gathers = [gather_copy(kind) for kind in range(3)]
    halos = [halo_copy(side, d) for side in range(2) for d in range(n_vec)]
    for c in gathers[:2] + halos:
        c.start()

    lane = lax.broadcasted_iota(jnp.int32, (8, 2 * rank), 1)
    low = lane < rank

    def swap(x):
        return pltpu.roll(x, rank, 1)

    load_b.wait()

    def skel_body(i, carry):
        for w in range(2):
            t = i * 2 + w
            sums = []
            for u in range(2):
                pair = t * 2 + u
                x = own_ref[pl.ds(pair * 2, 2)].reshape(16, 128)
                wt = basis[pl.ds(pl.multiple_of(pair * 128, 128), 128), :]
                r = dot_split(x, wt, NT)
                sums.append((r[:8], r[8:]))
            even = sums[0][0] + swap(sums[0][1])
            odd = swap(sums[1][0]) + sums[1][1]
            hp[t] = jnp.where(low, even, odd) * root_half
        return carry

    lax.fori_loop(0, leaves // 8, skel_body, 0)
    load_m.wait()

    def mat_pair(q):
        return mats[pl.ds(pl.multiple_of(q * 128, 128), 128), :]

    def up(off, nxt, t):
        r0 = dot_split(hp[off + 2 * t], mat_pair(off + 2 * t), NN)
        r1 = dot_split(hp[off + 2 * t + 1], mat_pair(off + 2 * t + 1), NN)
        hp[nxt + t] = jnp.where(low, swap(r0), r1) * root_half

    pairs = leaves // 4
    offs = []
    off = 0
    while pairs >= 1:
        offs.append((off, pairs))
        off += pairs
        pairs //= 2
    for (a, count), (b, half) in zip(offs[:-1], offs[1:]):
        if half > 4:
            def up_body(i, carry, a=a, b=b):
                for w in range(4):
                    up(a, b, i * 4 + w)
                return carry

            lax.fori_loop(0, half // 4, up_body, 0)
        else:
            for t in range(half):
                up(a, b, t)
    last = offs[-1][0]
    r = dot_split(hp[last], mat_pair(last), NN)
    skel = swap(r) * root_half
    top = mats[pl.ds((last + 1) * 128, rank), :]
    lift = dot_split(skel[:, :rank], top, NN)
    pay[li] = jnp.where(low, skel, lift)

    def pay_copy(d):
        return pltpu.make_async_remote_copy(
            src_ref=pay.at[li],
            dst_ref=pay.at[li],
            send_sem=pay_send.at[d],
            recv_sem=pay_recv.at[n_leaf - d],
            device_id=(lax.rem(li + d, n_leaf), vi),
            device_id_type=MESH,
        )

    pays = [pay_copy(d) for d in range(1, n_leaf)]
    for c in pays:
        c.start()

    gathers[0].wait_recv()
    gathers[2].start()
    counts = lax.broadcasted_iota(jnp.int32, (8, 128), 1).astype(f32).astype(bf16)

    def inverse_body(i, carry):
        for w in range(8):
            leaf = i * 8 + w
            hot = hot_of(order_ref[pl.ds(leaf, 1), :])
            inverse_ref[leaf] = lax.dot_general(counts, hot, NT, preferred_element_type=f32)
        return carry

    lax.fori_loop(0, leaves // 8, inverse_body, 0)
    load_o.wait()
    load_t.wait()
    for c in small:
        c.wait()
    for c in halos + gathers[1:]:
        c.wait_recv()
    for c in halos + gathers:
        c.wait_send()

    def split_body(i, carry):
        for w in range(4):
            e = i * 4 + w
            xs[e] = stacked(ext[:, e].reshape(n_vec * 8, 128))
        return carry

    lax.fori_loop(0, (leaves + 2 * W) // 4, split_body, 0)
    base = li * leaves - W
    slots = tiles.shape[1]
    piece = tiles.shape[2]

    def place(leaf, n):
        return jnp.clip(cols_ref[n, leaf] - base, 0, leaves + 2 * W - 1)

    def near_body(g, carry):
        outs = []
        for w in range(n_vec):
            leaf = g * n_vec + w
            x = jnp.concatenate([xs[place(leaf, n)] for n in range(slots)], axis=1)
            t = jnp.concatenate([stacked(tiles[leaf, n]) for n in range(slots)], axis=1)
            r = lax.dot_general(x, t, NT, preferred_element_type=f32)
            half = r.shape[0] // 2
            r = r[:half] + r[half:]
            outs.append(r[:, :piece] + r[:, piece:])
        nout[:, g] = jnp.concatenate(outs, axis=1).reshape(n_vec, 8, n_vec * piece)
        return carry

    lax.fori_loop(0, leaves // n_vec, near_body, 0)

    def near_copy(d):
        u = lax.rem(vi + d, n_vec)
        return pltpu.make_async_remote_copy(
            src_ref=nout.at[u],
            dst_ref=near_ref.at[vi],
            send_sem=near_send.at[d],
            recv_sem=near_recv.at[n_vec - d],
            device_id=(li, u),
            device_id_type=MESH,
        )

    nears = [near_copy(d) for d in range(1, n_vec)]
    for c in nears:
        c.start()
    keep = pltpu.make_async_copy(nout.at[vi], near_ref.at[vi], near_send.at[0])
    keep.start()

    for c in pays:
        c.wait_recv()
    for c in pays:
        c.wait_send()

    depth = n_leaf.bit_length() - 1

    def cross_at(c):
        return n_leaf - (n_leaf >> (c - 1))

    lifts = [pay[j] for j in range(n_leaf)]
    at = 0
    starts = {}
    for c in range(1, depth):
        nodes = [
            (lifts[2 * j] + lifts[2 * j + 1]) * root_half for j in range(len(lifts) // 2)
        ]
        nodes = [swap(x) if c == 1 else x for x in nodes]
        starts[c] = at
        for j, x in enumerate(nodes):
            hx[at + j] = x
        at += len(nodes)
        if c < depth - 1:
            lifts = []
            for j, x in enumerate(nodes):
                y = dot_split(x[:, :rank], cross_e_ref[cross_at(c) + j], NN)
                lifts.append(jnp.concatenate([y, y], axis=1))
    z = None
    for c in range(depth - 1, 0, -1):
        node = li >> c
        sibling = node + 1 - 2 * lax.rem(node, 2)
        spot = cross_at(c) + node
        a = cross_flags_ref[spot].astype(f32)
        g = dot_split(a * hx[starts[c] + sibling][:, :rank], cross_c_ref[spot], NT)
        z = g if z is None else g + dot_split(z, cross_e_ref[spot], NT)
    sibling = li + 1 - 2 * lax.rem(li, 2)
    a = flags_ref[0, 2 * (last + 1)].astype(f32)
    x = jnp.where(low, a * pay[sibling], jnp.concatenate([z, z], axis=1))
    z = dot_split(x, top, NT)
    z = jnp.concatenate([z, z], axis=1)

    def down(q, parent):
        h = hp[q]
        a0 = flags_ref[0, 2 * q].astype(f32)
        a1 = flags_ref[0, 2 * q + 1].astype(f32)
        x0 = jnp.where(low, a0 * swap(h), parent)
        x1 = jnp.where(low, a1 * h, parent)
        r = dot_split(jnp.concatenate([x0, x1], axis=0), mat_pair(q), NT)
        zp[q] = jnp.where(low, r[:8], r[8:])

    down(last, z)
    for (a, count), (b, half) in list(zip(offs[:-1], offs[1:]))[::-1]:
        def down_one(t, a=a, b=b):
            p = zp[b + t]
            down(a + 2 * t, swap(p))
            down(a + 2 * t + 1, p)

        if half > 4:
            def down_body(i, carry, down_one=down_one):
                for w in range(4):
                    down_one(i * 4 + w)
                return carry

            lax.fori_loop(0, half // 4, down_body, 0)
        else:
            for t in range(half):
                down_one(t)

    def far_body(i, carry):
        for w in range(2):
            t = i * 2 + w
            p = zp[t]
            s = swap(p)
            zero = jnp.zeros_like(p)
            for u in range(2):
                pair = 2 * t + u
                first, second = (p, s) if u == 0 else (s, p)
                x = jnp.concatenate(
                    [jnp.where(low, first, zero), jnp.where(low, zero, second)], axis=0
                )
                wt = basis[pl.ds(pl.multiple_of(pair * 128, 128), 128), :]
                r = dot_split(x, wt, NN)
                far_ref[2 * pair] = r[:8]
                far_ref[2 * pair + 1] = r[8:]
        return carry

    lax.fori_loop(0, leaves // 8, far_body, 0)
    keep.wait()
    for c in nears:
        c.wait_recv()
    for c in nears:
        c.wait_send()


def local(
    panels,
    near_tiles,
    near_cols,
    leaf_order,
    leaf_basis,
    local_mats,
    local_flags,
    cross_coupling,
    cross_transfer,
    cross_flags,
):
    rows = panels.shape[0]
    leaves, rank, size = leaf_basis.shape
    n_leaf = lax.axis_size("leaf")
    n_vec = lax.axis_size("vec")
    vmem = pl.BlockSpec(memory_space=pltpu.VMEM)
    hbm = pl.BlockSpec(memory_space=pl.ANY)
    ordered = pl.pallas_call(
        order_kernel,
        out_shape=jax.ShapeDtypeStruct((leaves, rows, size), f32),
        in_specs=[vmem, vmem],
        out_specs=vmem,
        name="order",
    )(panels, leaf_order)
    basis2 = leaf_basis.reshape(leaves * rank, size)
    mats2 = local_mats.reshape(local_mats.shape[1] * rank, 2 * rank)
    groups = leaves // n_vec
    dma = pltpu.SemaphoreType.DMA
    far, near, inverse = pl.pallas_call(
        functools.partial(main_kernel, n_leaf, n_vec),
        out_shape=(
            jax.ShapeDtypeStruct((leaves, rows, size), f32),
            jax.ShapeDtypeStruct((n_vec, groups, rows, size), f32),
            jax.ShapeDtypeStruct((leaves, rows, size), f32),
        ),
        in_specs=[vmem, vmem] + [hbm] * 8,
        out_specs=(vmem, vmem, vmem),
        scratch_shapes=[
            pltpu.SMEM(near_cols.shape[::-1], jnp.int32),
            pltpu.SMEM(local_flags.shape, jnp.int32),
            pltpu.SMEM(cross_flags.shape, jnp.int32),
            pltpu.VMEM(cross_coupling.shape, f32),
            pltpu.VMEM(cross_transfer.shape, f32),
            pltpu.VMEM(near_tiles.shape, f32),
            pltpu.VMEM(basis2.shape, f32),
            pltpu.VMEM(mats2.shape, f32),
            pltpu.VMEM((n_vec, leaves + 2 * W, rows, size), f32),
            pltpu.VMEM((leaves + 2 * W, 2 * n_vec * rows, size), bf16),
            pltpu.VMEM((leaves // 2, rows, size), f32),
            pltpu.VMEM((leaves // 2, rows, size), f32),
            pltpu.VMEM((n_leaf, rows, 2 * rank), f32),
            pltpu.VMEM((n_leaf, rows, 2 * rank), f32),
            pltpu.VMEM((n_vec, groups, rows, size), f32),
            dma((9,)),
            dma((n_vec,)),
            dma((n_vec,)),
            dma((2, n_vec)),
            dma((2, n_vec)),
            dma((n_leaf,)),
            dma((n_leaf,)),
            dma((n_vec,)),
            dma((n_vec,)),
        ],
        compiler_params=pltpu.CompilerParams(
            collective_id=0, has_side_effects=True, vmem_limit_bytes=61 * 1024 * 1024
        ),
        name="tree",
    )(
        ordered,
        leaf_order,
        near_cols.T,
        local_flags,
        cross_flags,
        cross_coupling,
        cross_transfer,
        near_tiles,
        basis2,
        mats2,
    )
    return pl.pallas_call(
        restore_kernel,
        out_shape=jax.ShapeDtypeStruct(panels.shape, f32),
        in_specs=[vmem, vmem, vmem],
        out_specs=vmem,
        name="restore",
    )(far, near, inverse)


def solution(mesh):
    return jax.shard_map(
        local,
        mesh=mesh,
        in_specs=(
            P("vec", "leaf"),
            P("leaf", None, "vec", None),
            P("leaf", None),
            P("leaf", None),
            P("leaf", None, None),
            P("leaf", None, None, None),
            P("leaf", None),
            P(),
            P(),
            P(),
        ),
        out_specs=P("vec", "leaf"),
        check_vma=False,
    )
```

```python
import functools
import math

import jax
import jax.numpy as jnp
from jax import lax
from jax.experimental import pallas as pl
from jax.experimental.pallas import tpu as pltpu
from jax.sharding import PartitionSpec as P

W = 8
f32 = jnp.float32
bf16 = jnp.bfloat16
root_half = 1.0 / math.sqrt(2.0)
MESH = pl.DeviceIdType.MESH
NN = (((1,), (0,)), ((), ()))
NT = (((1,), (1,)), ((), ()))


def halves(x):
    high = x.astype(bf16).astype(f32)
    return high, x - high


def stacked(x):
    return jnp.concatenate(halves(x), axis=0).astype(bf16)


def dot_split(x, w, dims):
    rows = x.shape[0]
    lhs = stacked(x)
    high = w.astype(bf16)
    low = (w - high.astype(f32)).astype(bf16)
    r = lax.dot_general(lhs, high, dims, preferred_element_type=f32) + lax.dot_general(
        lhs, low, dims, preferred_element_type=f32
    )
    return r[:rows] + r[rows:]


def hot_of(order_row):
    size = order_row.shape[1]
    rows = lax.broadcasted_iota(jnp.int32, (size, size), 0)
    return jnp.where(rows == order_row, 1.0, 0.0).astype(bf16)


def order_kernel(panels_ref, order_ref, out_ref):
    leaves, size = order_ref.shape
    span = 8

    def body(i, carry):
        for u in range(span):
            leaf = i * span + u
            x = panels_ref[:, pl.ds(pl.multiple_of(leaf * size, size), size)]
            spots = jnp.broadcast_to(order_ref[pl.ds(leaf, 1), :], x.shape)
            out_ref[leaf] = jnp.take_along_axis(x, spots, axis=1)
        return carry

    lax.fori_loop(0, leaves // span, body, 0)


def restore_kernel(far_ref, near_ref, inverse_ref, out_ref):
    leaves, _, size = far_ref.shape
    n_vec = near_ref.shape[0]
    piece = size // n_vec
    rows = out_ref.shape[0]
    block = lax.broadcasted_iota(jnp.int32, (rows, size), 1) // piece

    def body(g, carry):
        parts = [near_ref[v, g] for v in range(n_vec)]
        for u in range(n_vec):
            leaf = g * n_vec + u
            near = parts[0] if u == 0 else pltpu.roll(parts[0], (size - u * piece), 1)
            for v in range(1, n_vec):
                shift = ((v - u) * piece) % size
                moved = parts[v] if shift == 0 else pltpu.roll(parts[v], shift, 1)
                near = jnp.where(block == v, moved, near)
            combined = near + far_ref[leaf]
            spots = inverse_ref[leaf].astype(jnp.int32)
            out_ref[:, pl.ds(pl.multiple_of(leaf * size, size), size)] = jnp.take_along_axis(
                combined, spots, axis=1
            )
        return carry

    lax.fori_loop(0, leaves // n_vec, body, 0)


def main_kernel(
    n_leaf,
    n_vec,
    own_ref,
    order_ref,
    cols_hbm,
    flags_hbm,
    cross_flags_hbm,
    cross_c_hbm,
    cross_e_hbm,
    tiles_hbm,
    basis_hbm,
    mats_hbm,
    far_ref,
    near_ref,
    inverse_ref,
    cols_ref,
    flags_ref,
    cross_flags_ref,
    cross_c_ref,
    cross_e_ref,
    tiles,
    basis,
    mats,
    ext,
    xs,
    hp,
    zp,
    pay,
    hx,
    nout,
    load_sem,
    gs_send,
    gs_recv,
    halo_send,
    halo_recv,
    pay_send,
    pay_recv,
    near_send,
    near_recv,
):
    leaves = own_ref.shape[0]
    rank = 64
    li = lax.axis_index("leaf")
    vi = lax.axis_index("vec")
    load_b = pltpu.make_async_copy(basis_hbm, basis, load_sem.at[0])
    load_m = pltpu.make_async_copy(mats_hbm, mats, load_sem.at[1])
    load_t = pltpu.make_async_copy(tiles_hbm, tiles, load_sem.at[2])
    load_o = pltpu.make_async_copy(own_ref, ext.at[vi, pl.ds(W, leaves)], load_sem.at[3])
    load_b.start()
    load_m.start()
    load_t.start()
    load_o.start()
    small = [
        pltpu.make_async_copy(src, dst, load_sem.at[4 + i])
        for i, (src, dst) in enumerate(
            [
                (cols_hbm, cols_ref),
                (flags_hbm, flags_ref),
                (cross_flags_hbm, cross_flags_ref),
                (cross_c_hbm, cross_c_ref),
                (cross_e_hbm, cross_e_ref),
            ]
        )
    ]
    for c in small:
        c.start()

    right = lax.rem(li + 1, n_leaf)
    left = lax.rem(li + n_leaf - 1, n_leaf)
    barrier = pltpu.get_barrier_semaphore()
    greeted = 0
    for d in range(1, n_vec):
        pl.semaphore_signal(
            barrier, inc=1, device_id=(li, lax.rem(vi + d, n_vec)), device_id_type=MESH
        )
        greeted += 1
    for d in range(1, n_leaf):
        pl.semaphore_signal(
            barrier, inc=1, device_id=(lax.rem(li + d, n_leaf), vi), device_id_type=MESH
        )
        greeted += 1
    pl.semaphore_wait(barrier, greeted)

    beside = vi + 1 - 2 * lax.rem(vi, 2)
    across = lax.rem(vi + 2, n_vec)

    def gather_copy(kind):
        block = ext.at[across if kind == 2 else vi, pl.ds(W, leaves)]
        return pltpu.make_async_remote_copy(
            src_ref=block if kind == 2 else own_ref,
            dst_ref=block,
            send_sem=gs_send.at[kind],
            recv_sem=gs_recv.at[kind],
            device_id=(li, across if kind == 0 else beside),
            device_id_type=MESH,
        )

    rims = (0, leaves + W)

    def halo_copy(side):
        return pltpu.make_async_remote_copy(
            src_ref=own_ref.at[pl.ds(leaves - W if side == 0 else 0, W)],
            dst_ref=ext.at[vi, pl.ds(rims[side], W)],
            send_sem=halo_send.at[side, 3],
            recv_sem=halo_recv.at[side, 3],
            device_id=(right if side == 0 else left, vi),
            device_id_type=MESH,
        )

    def rim_copy(side, kind):
        block = ext.at[across if kind == 2 else vi, pl.ds(rims[side], W)]
        return pltpu.make_async_remote_copy(
            src_ref=block,
            dst_ref=block,
            send_sem=halo_send.at[side, kind],
            recv_sem=halo_recv.at[side, kind],
            device_id=(li, across if kind == 0 else beside),
            device_id_type=MESH,
        )

    assert n_vec == 4
    gathers = [gather_copy(kind) for kind in range(3)]
    halos = [halo_copy(side) for side in range(2)]
    rim_copies = [[rim_copy(side, kind) for side in range(2)] for kind in range(3)]
    for c in halos + gathers[:2]:
        c.start()

    lane = lax.broadcasted_iota(jnp.int32, (8, 2 * rank), 1)
    low = lane < rank

    def swap(x):
        return pltpu.roll(x, rank, 1)

    load_b.wait()

    def skel_body(i, carry):
        for w in range(2):
            t = i * 2 + w
            sums = []
            for u in range(2):
                pair = t * 2 + u
                x = own_ref[pl.ds(pair * 2, 2)].reshape(16, 128)
                wt = basis[pl.ds(pl.multiple_of(pair * 128, 128), 128), :]
                r = dot_split(x, wt, NT)
                sums.append((r[:8], r[8:]))
            even = sums[0][0] + swap(sums[0][1])
            odd = swap(sums[1][0]) + sums[1][1]
            hp[t] = jnp.where(low, even, odd) * root_half
        return carry

    lax.fori_loop(0, leaves // 8, skel_body, 0)
    for c in halos:
        c.wait_recv()
    for c in rim_copies[0] + rim_copies[1]:
        c.start()
    load_m.wait()

    def mat_pair(q):
        return mats[pl.ds(pl.multiple_of(q * 128, 128), 128), :]

    def up(off, nxt, t):
        r0 = dot_split(hp[off + 2 * t], mat_pair(off + 2 * t), NN)
        r1 = dot_split(hp[off + 2 * t + 1], mat_pair(off + 2 * t + 1), NN)
        hp[nxt + t] = jnp.where(low, swap(r0), r1) * root_half

    pairs = leaves // 4
    offs = []
    off = 0
    while pairs >= 1:
        offs.append((off, pairs))
        off += pairs
        pairs //= 2
    for (a, count), (b, half) in zip(offs[:-1], offs[1:]):
        if half > 4:
            def up_body(i, carry, a=a, b=b):
                for w in range(4):
                    up(a, b, i * 4 + w)
                return carry

            lax.fori_loop(0, half // 4, up_body, 0)
        else:
            for t in range(half):
                up(a, b, t)
    last = offs[-1][0]
    r = dot_split(hp[last], mat_pair(last), NN)
    skel = swap(r) * root_half
    top = mats[pl.ds((last + 1) * 128, rank), :]
    lift = dot_split(skel[:, :rank], top, NN)
    pay[li] = jnp.where(low, skel, lift)

    def pay_copy(d):
        return pltpu.make_async_remote_copy(
            src_ref=pay.at[li],
            dst_ref=pay.at[li],
            send_sem=pay_send.at[d],
            recv_sem=pay_recv.at[n_leaf - d],
            device_id=(lax.rem(li + d, n_leaf), vi),
            device_id_type=MESH,
        )

    pays = [pay_copy(d) for d in range(1, n_leaf)]
    for c in pays:
        c.start()

    counts = lax.broadcasted_iota(jnp.int32, (8, 128), 1).astype(f32).astype(bf16)

    def inverse_body(i, carry):
        for w in range(8):
            leaf = i * 8 + w
            hot = hot_of(order_ref[pl.ds(leaf, 1), :])
            inverse_ref[leaf] = lax.dot_general(counts, hot, NT, preferred_element_type=f32)
        return carry

    lax.fori_loop(0, leaves // 8, inverse_body, 0)
    for c in rim_copies[0]:
        c.wait_recv()
    for c in rim_copies[2]:
        c.start()
    gathers[0].wait_recv()
    gathers[2].start()
    for c in small:
        c.wait()
    for c in pays:
        c.wait_recv()
    for c in pays:
        c.wait_send()

    depth = n_leaf.bit_length() - 1

    def cross_at(c):
        return n_leaf - (n_leaf >> (c - 1))

    lifts = [pay[j] for j in range(n_leaf)]
    at = 0
    starts = {}
    for c in range(1, depth):
        nodes = [
            (lifts[2 * j] + lifts[2 * j + 1]) * root_half for j in range(len(lifts) // 2)
        ]
        nodes = [swap(x) if c == 1 else x for x in nodes]
        starts[c] = at
        for j, x in enumerate(nodes):
            hx[at + j] = x
        at += len(nodes)
        if c < depth - 1:
            lifts = []
            for j, x in enumerate(nodes):
                y = dot_split(x[:, :rank], cross_e_ref[cross_at(c) + j], NN)
                lifts.append(jnp.concatenate([y, y], axis=1))
    z = None
    for c in range(depth - 1, 0, -1):
        node = li >> c
        sibling = node + 1 - 2 * lax.rem(node, 2)
        spot = cross_at(c) + node
        a = cross_flags_ref[spot].astype(f32)
        g = dot_split(a * hx[starts[c] + sibling][:, :rank], cross_c_ref[spot], NT)
        z = g if z is None else g + dot_split(z, cross_e_ref[spot], NT)
    sibling = li + 1 - 2 * lax.rem(li, 2)
    a = flags_ref[0, 2 * (last + 1)].astype(f32)
    x = jnp.where(low, a * pay[sibling], jnp.concatenate([z, z], axis=1))
    z = dot_split(x, top, NT)
    z = jnp.concatenate([z, z], axis=1)

    def down(q, parent):
        h = hp[q]
        a0 = flags_ref[0, 2 * q].astype(f32)
        a1 = flags_ref[0, 2 * q + 1].astype(f32)
        x0 = jnp.where(low, a0 * swap(h), parent)
        x1 = jnp.where(low, a1 * h, parent)
        r = dot_split(jnp.concatenate([x0, x1], axis=0), mat_pair(q), NT)
        zp[q] = jnp.where(low, r[:8], r[8:])

    down(last, z)
    for (a, count), (b, half) in list(zip(offs[:-1], offs[1:]))[::-1]:
        def down_one(t, a=a, b=b):
            p = zp[b + t]
            down(a + 2 * t, swap(p))
            down(a + 2 * t + 1, p)

        if half > 4:
            def down_body(i, carry, down_one=down_one):
                for w in range(4):
                    down_one(i * 4 + w)
                return carry

            lax.fori_loop(0, half // 4, down_body, 0)
        else:
            for t in range(half):
                down_one(t)

    load_o.wait()
    load_t.wait()
    for c in gathers[1:] + rim_copies[1] + rim_copies[2]:
        c.wait_recv()
    for c in halos + gathers + rim_copies[0] + rim_copies[1] + rim_copies[2]:
        c.wait_send()

    def split_body(i, carry):
        for w in range(4):
            e = i * 4 + w
            xs[e] = stacked(ext[:, e].reshape(n_vec * 8, 128))
        return carry

    lax.fori_loop(0, (leaves + 2 * W) // 4, split_body, 0)
    base = li * leaves - W
    slots = tiles.shape[1]
    piece = tiles.shape[2]

    def place(leaf, n):
        return jnp.clip(cols_ref[n, leaf] - base, 0, leaves + 2 * W - 1)

    def near_body(g, carry):
        outs = []
        for w in range(n_vec):
            leaf = g * n_vec + w
            x = jnp.concatenate([xs[place(leaf, n)] for n in range(slots)], axis=1)
            t = jnp.concatenate([stacked(tiles[leaf, n]) for n in range(slots)], axis=1)
            r = lax.dot_general(x, t, NT, preferred_element_type=f32)
            half = r.shape[0] // 2
            r = r[:half] + r[half:]
            outs.append(r[:, :piece] + r[:, piece:])
        nout[:, g] = jnp.concatenate(outs, axis=1).reshape(n_vec, 8, n_vec * piece)
        return carry

    half_groups = leaves // n_vec // 2

    def near_copy(d, part):
        u = lax.rem(vi + d, n_vec)
        span = pl.ds(part * half_groups, half_groups)
        return pltpu.make_async_remote_copy(
            src_ref=nout.at[u, span],
            dst_ref=near_ref.at[vi, span],
            send_sem=near_send.at[part, d],
            recv_sem=near_recv.at[part, n_vec - d],
            device_id=(li, u),
            device_id_type=MESH,
        )

    nears = []
    for part in range(2):
        lax.fori_loop(part * half_groups, (part + 1) * half_groups, near_body, 0)
        batch = [near_copy(d, part) for d in (2, 1, 3)]
        for c in batch:
            c.start()
        nears += batch
    keep = pltpu.make_async_copy(nout.at[vi], near_ref.at[vi], near_send.at[0, 0])
    keep.start()

    def far_body(i, carry):
        for w in range(2):
            t = i * 2 + w
            p = zp[t]
            s = swap(p)
            zero = jnp.zeros_like(p)
            for u in range(2):
                pair = 2 * t + u
                first, second = (p, s) if u == 0 else (s, p)
                x = jnp.concatenate(
                    [jnp.where(low, first, zero), jnp.where(low, zero, second)], axis=0
                )
                wt = basis[pl.ds(pl.multiple_of(pair * 128, 128), 128), :]
                r = dot_split(x, wt, NN)
                far_ref[2 * pair] = r[:8]
                far_ref[2 * pair + 1] = r[8:]
        return carry

    lax.fori_loop(0, leaves // 8, far_body, 0)
    keep.wait()
    for c in nears:
        c.wait_recv()
    for c in nears:
        c.wait_send()


def local(
    panels,
    near_tiles,
    near_cols,
    leaf_order,
    leaf_basis,
    local_mats,
    local_flags,
    cross_coupling,
    cross_transfer,
    cross_flags,
):
    rows = panels.shape[0]
    leaves, rank, size = leaf_basis.shape
    n_leaf = lax.axis_size("leaf")
    n_vec = lax.axis_size("vec")
    vmem = pl.BlockSpec(memory_space=pltpu.VMEM)
    hbm = pl.BlockSpec(memory_space=pl.ANY)
    ordered = pl.pallas_call(
        order_kernel,
        out_shape=jax.ShapeDtypeStruct((leaves, rows, size), f32),
        in_specs=[vmem, vmem],
        out_specs=vmem,
        name="order",
    )(panels, leaf_order)
    basis2 = leaf_basis.reshape(leaves * rank, size)
    mats2 = local_mats.reshape(local_mats.shape[1] * rank, 2 * rank)
    groups = leaves // n_vec
    dma = pltpu.SemaphoreType.DMA
    far, near, inverse = pl.pallas_call(
        functools.partial(main_kernel, n_leaf, n_vec),
        out_shape=(
            jax.ShapeDtypeStruct((leaves, rows, size), f32),
            jax.ShapeDtypeStruct((n_vec, groups, rows, size), f32),
            jax.ShapeDtypeStruct((leaves, rows, size), f32),
        ),
        in_specs=[vmem, vmem] + [hbm] * 8,
        out_specs=(vmem, vmem, vmem),
        scratch_shapes=[
            pltpu.SMEM(near_cols.shape[::-1], jnp.int32),
            pltpu.SMEM(local_flags.shape, jnp.int32),
            pltpu.SMEM(cross_flags.shape, jnp.int32),
            pltpu.VMEM(cross_coupling.shape, f32),
            pltpu.VMEM(cross_transfer.shape, f32),
            pltpu.VMEM(near_tiles.shape, f32),
            pltpu.VMEM(basis2.shape, f32),
            pltpu.VMEM(mats2.shape, f32),
            pltpu.VMEM((n_vec, leaves + 2 * W, rows, size), f32),
            pltpu.VMEM((leaves + 2 * W, 2 * n_vec * rows, size), bf16),
            pltpu.VMEM((leaves // 2, rows, size), f32),
            pltpu.VMEM((leaves // 2, rows, size), f32),
            pltpu.VMEM((n_leaf, rows, 2 * rank), f32),
            pltpu.VMEM((n_leaf, rows, 2 * rank), f32),
            pltpu.VMEM((n_vec, groups, rows, size), f32),
            dma((9,)),
            dma((n_vec,)),
            dma((n_vec,)),
            dma((2, n_vec)),
            dma((2, n_vec)),
            dma((n_leaf,)),
            dma((n_leaf,)),
            dma((2, n_vec)),
            dma((2, n_vec)),
        ],
        compiler_params=pltpu.CompilerParams(
            collective_id=0, has_side_effects=True, vmem_limit_bytes=61 * 1024 * 1024
        ),
        name="tree",
    )(
        ordered,
        leaf_order,
        near_cols.T,
        local_flags,
        cross_flags,
        cross_coupling,
        cross_transfer,
        near_tiles,
        basis2,
        mats2,
    )
    return pl.pallas_call(
        restore_kernel,
        out_shape=jax.ShapeDtypeStruct(panels.shape, f32),
        in_specs=[vmem, vmem, vmem],
        out_specs=vmem,
        name="restore",
    )(far, near, inverse)


def solution(mesh):
    return jax.shard_map(
        local,
        mesh=mesh,
        in_specs=(
            P("vec", "leaf"),
            P("leaf", None, "vec", None),
            P("leaf", None),
            P("leaf", None),
            P("leaf", None, None),
            P("leaf", None, None, None),
            P("leaf", None),
            P(),
            P(),
            P(),
        ),
        out_specs=P("vec", "leaf"),
        check_vma=False,
    )
```

```python
import functools
import math

import jax
import jax.numpy as jnp
from jax import lax
from jax.experimental import pallas as pl
from jax.experimental.pallas import tpu as pltpu
from jax.sharding import PartitionSpec as P

W = 8
f32 = jnp.float32
bf16 = jnp.bfloat16
root_half = 1.0 / math.sqrt(2.0)
MESH = pl.DeviceIdType.MESH
NN = (((1,), (0,)), ((), ()))
NT = (((1,), (1,)), ((), ()))


def halves(x):
    high = x.astype(bf16).astype(f32)
    return high, x - high


def stacked(x):
    return jnp.concatenate(halves(x), axis=0).astype(bf16)


def dot_split(x, w, dims):
    rows = x.shape[0]
    lhs = stacked(x)
    high = w.astype(bf16)
    low = (w - high.astype(f32)).astype(bf16)
    r = lax.dot_general(lhs, high, dims, preferred_element_type=f32) + lax.dot_general(
        lhs, low, dims, preferred_element_type=f32
    )
    return r[:rows] + r[rows:]


def hot_of(order_row):
    size = order_row.shape[1]
    rows = lax.broadcasted_iota(jnp.int32, (size, size), 0)
    return jnp.where(rows == order_row, 1.0, 0.0).astype(bf16)


def order_kernel(panels_ref, order_ref, out_ref):
    leaves, size = order_ref.shape
    span = 32

    def body(i, carry):
        for u in range(span):
            leaf = i * span + u
            x = panels_ref[:, pl.ds(pl.multiple_of(leaf * size, size), size)]
            spots = jnp.broadcast_to(order_ref[pl.ds(leaf, 1), :], x.shape)
            out_ref[leaf] = jnp.take_along_axis(x, spots, axis=1)
        return carry

    lax.fori_loop(0, leaves // span, body, 0)


def restore_kernel(far_ref, near_ref, inverse_ref, out_ref):
    leaves, _, size = far_ref.shape
    n_vec = near_ref.shape[0]
    piece = size // n_vec
    rows = out_ref.shape[0]
    block = lax.broadcasted_iota(jnp.int32, (rows, size), 1) // piece

    def group(g):
        parts = [near_ref[v, g] for v in range(n_vec)]
        for u in range(n_vec):
            leaf = g * n_vec + u
            near = parts[0] if u == 0 else pltpu.roll(parts[0], (size - u * piece), 1)
            for v in range(1, n_vec):
                shift = ((v - u) * piece) % size
                moved = parts[v] if shift == 0 else pltpu.roll(parts[v], shift, 1)
                near = jnp.where(block == v, moved, near)
            combined = near + far_ref[leaf]
            spots = inverse_ref[leaf].astype(jnp.int32)
            out_ref[:, pl.ds(pl.multiple_of(leaf * size, size), size)] = jnp.take_along_axis(
                combined, spots, axis=1
            )

    def body(i, carry):
        for w in range(4):
            group(i * 4 + w)
        return carry

    lax.fori_loop(0, leaves // n_vec // 4, body, 0)


def main_kernel(
    n_leaf,
    n_vec,
    own_ref,
    order_ref,
    cols_hbm,
    flags_hbm,
    cross_flags_hbm,
    cross_c_hbm,
    cross_e_hbm,
    tiles_hbm,
    basis_hbm,
    mats_hbm,
    far_ref,
    near_ref,
    inverse_ref,
    cols_ref,
    flags_ref,
    cross_flags_ref,
    cross_c_ref,
    cross_e_ref,
    tiles,
    basis,
    mats,
    ext,
    xs,
    hp,
    zp,
    pay,
    hx,
    nout,
    load_sem,
    gs_send,
    gs_recv,
    halo_send,
    halo_recv,
    pay_send,
    pay_recv,
    near_send,
    near_recv,
):
    leaves = own_ref.shape[0]
    rank = 64
    li = lax.axis_index("leaf")
    vi = lax.axis_index("vec")
    load_b = pltpu.make_async_copy(basis_hbm, basis, load_sem.at[0])
    load_m = pltpu.make_async_copy(mats_hbm, mats, load_sem.at[1])
    load_t = pltpu.make_async_copy(tiles_hbm, tiles, load_sem.at[2])
    load_o = pltpu.make_async_copy(own_ref, ext.at[vi, pl.ds(W, leaves)], load_sem.at[3])
    load_b.start()
    load_m.start()
    load_t.start()
    load_o.start()
    small = [
        pltpu.make_async_copy(src, dst, load_sem.at[4 + i])
        for i, (src, dst) in enumerate(
            [
                (cols_hbm, cols_ref),
                (flags_hbm, flags_ref),
                (cross_flags_hbm, cross_flags_ref),
                (cross_c_hbm, cross_c_ref),
                (cross_e_hbm, cross_e_ref),
            ]
        )
    ]
    for c in small:
        c.start()

    right = lax.rem(li + 1, n_leaf)
    left = lax.rem(li + n_leaf - 1, n_leaf)
    barrier = pltpu.get_barrier_semaphore()
    greeted = 0
    for d in range(1, n_vec):
        pl.semaphore_signal(
            barrier, inc=1, device_id=(li, lax.rem(vi + d, n_vec)), device_id_type=MESH
        )
        greeted += 1
    for d in range(1, n_leaf):
        pl.semaphore_signal(
            barrier, inc=1, device_id=(lax.rem(li + d, n_leaf), vi), device_id_type=MESH
        )
        greeted += 1
    pl.semaphore_wait(barrier, greeted)

    beside = vi + 1 - 2 * lax.rem(vi, 2)
    across = lax.rem(vi + 2, n_vec)

    def gather_copy(kind):
        block = ext.at[across if kind == 2 else vi, pl.ds(W, leaves)]
        return pltpu.make_async_remote_copy(
            src_ref=block if kind == 2 else own_ref,
            dst_ref=block,
            send_sem=gs_send.at[kind],
            recv_sem=gs_recv.at[kind],
            device_id=(li, across if kind == 0 else beside),
            device_id_type=MESH,
        )

    rims = (0, leaves + W)

    def halo_copy(side):
        return pltpu.make_async_remote_copy(
            src_ref=own_ref.at[pl.ds(leaves - W if side == 0 else 0, W)],
            dst_ref=ext.at[vi, pl.ds(rims[side], W)],
            send_sem=halo_send.at[side, 3],
            recv_sem=halo_recv.at[side, 3],
            device_id=(right if side == 0 else left, vi),
            device_id_type=MESH,
        )

    def rim_copy(side, kind):
        block = ext.at[across if kind == 2 else vi, pl.ds(rims[side], W)]
        return pltpu.make_async_remote_copy(
            src_ref=block,
            dst_ref=block,
            send_sem=halo_send.at[side, kind],
            recv_sem=halo_recv.at[side, kind],
            device_id=(li, across if kind == 0 else beside),
            device_id_type=MESH,
        )

    assert n_vec == 4
    gathers = [gather_copy(kind) for kind in range(3)]
    halos = [halo_copy(side) for side in range(2)]
    rim_copies = [[rim_copy(side, kind) for side in range(2)] for kind in range(3)]
    for c in halos + gathers[:2]:
        c.start()

    lane = lax.broadcasted_iota(jnp.int32, (8, 2 * rank), 1)
    low = lane < rank

    def swap(x):
        return pltpu.roll(x, rank, 1)

    load_b.wait()

    def skel_body(i, carry):
        for w in range(4):
            t = i * 4 + w
            sums = []
            for u in range(2):
                pair = t * 2 + u
                x = own_ref[pl.ds(pair * 2, 2)].reshape(16, 128)
                wt = basis[pl.ds(pl.multiple_of(pair * 128, 128), 128), :]
                r = dot_split(x, wt, NT)
                sums.append((r[:8], r[8:]))
            even = sums[0][0] + swap(sums[0][1])
            odd = swap(sums[1][0]) + sums[1][1]
            hp[t] = jnp.where(low, even, odd) * root_half
        return carry

    lax.fori_loop(0, leaves // 16, skel_body, 0)
    for c in halos:
        c.wait_recv()
    for c in rim_copies[0] + rim_copies[1]:
        c.start()
    load_m.wait()

    def mat_pair(q):
        return mats[pl.ds(pl.multiple_of(q * 128, 128), 128), :]

    def up(off, nxt, t):
        r0 = dot_split(hp[off + 2 * t], mat_pair(off + 2 * t), NN)
        r1 = dot_split(hp[off + 2 * t + 1], mat_pair(off + 2 * t + 1), NN)
        hp[nxt + t] = jnp.where(low, swap(r0), r1) * root_half

    pairs = leaves // 4
    offs = []
    off = 0
    while pairs >= 1:
        offs.append((off, pairs))
        off += pairs
        pairs //= 2
    for (a, count), (b, half) in zip(offs[:-1], offs[1:]):
        if half > 8:
            def up_body(i, carry, a=a, b=b):
                for w in range(4):
                    up(a, b, i * 4 + w)
                return carry

            lax.fori_loop(0, half // 4, up_body, 0)
        else:
            for t in range(half):
                up(a, b, t)
    last = offs[-1][0]
    r = dot_split(hp[last], mat_pair(last), NN)
    skel = swap(r) * root_half
    top = mats[pl.ds((last + 1) * 128, rank), :]
    lift = dot_split(skel[:, :rank], top, NN)
    pay[li] = jnp.where(low, skel, lift)

    def pay_copy(d):
        return pltpu.make_async_remote_copy(
            src_ref=pay.at[li],
            dst_ref=pay.at[li],
            send_sem=pay_send.at[d],
            recv_sem=pay_recv.at[n_leaf - d],
            device_id=(lax.rem(li + d, n_leaf), vi),
            device_id_type=MESH,
        )

    pays = [pay_copy(d) for d in range(1, n_leaf)]
    for c in pays:
        c.start()

    counts = lax.broadcasted_iota(jnp.int32, (8, 128), 1).astype(f32).astype(bf16)

    def inverse_body(i, carry):
        for w in range(16):
            leaf = i * 16 + w
            hot = hot_of(order_ref[pl.ds(leaf, 1), :])
            inverse_ref[leaf] = lax.dot_general(counts, hot, NT, preferred_element_type=f32)
        return carry

    lax.fori_loop(0, leaves // 16, inverse_body, 0)
    for c in rim_copies[0]:
        c.wait_recv()
    for c in rim_copies[2]:
        c.start()
    gathers[0].wait_recv()
    gathers[2].start()
    for c in small:
        c.wait()
    for c in pays:
        c.wait_recv()
    for c in pays:
        c.wait_send()

    depth = n_leaf.bit_length() - 1

    def cross_at(c):
        return n_leaf - (n_leaf >> (c - 1))

    lifts = [pay[j] for j in range(n_leaf)]
    at = 0
    starts = {}
    for c in range(1, depth):
        nodes = [
            (lifts[2 * j] + lifts[2 * j + 1]) * root_half for j in range(len(lifts) // 2)
        ]
        nodes = [swap(x) if c == 1 else x for x in nodes]
        starts[c] = at
        for j, x in enumerate(nodes):
            hx[at + j] = x
        at += len(nodes)
        if c < depth - 1:
            lifts = []
            for j, x in enumerate(nodes):
                y = dot_split(x[:, :rank], cross_e_ref[cross_at(c) + j], NN)
                lifts.append(jnp.concatenate([y, y], axis=1))
    z = None
    for c in range(depth - 1, 0, -1):
        node = li >> c
        sibling = node + 1 - 2 * lax.rem(node, 2)
        spot = cross_at(c) + node
        a = cross_flags_ref[spot].astype(f32)
        g = dot_split(a * hx[starts[c] + sibling][:, :rank], cross_c_ref[spot], NT)
        z = g if z is None else g + dot_split(z, cross_e_ref[spot], NT)
    sibling = li + 1 - 2 * lax.rem(li, 2)
    a = flags_ref[0, 2 * (last + 1)].astype(f32)
    x = jnp.where(low, a * pay[sibling], jnp.concatenate([z, z], axis=1))
    z = dot_split(x, top, NT)
    z = jnp.concatenate([z, z], axis=1)

    def down(q, parent):
        h = hp[q]
        a0 = flags_ref[0, 2 * q].astype(f32)
        a1 = flags_ref[0, 2 * q + 1].astype(f32)
        x0 = jnp.where(low, a0 * swap(h), parent)
        x1 = jnp.where(low, a1 * h, parent)
        r = dot_split(jnp.concatenate([x0, x1], axis=0), mat_pair(q), NT)
        zp[q] = jnp.where(low, r[:8], r[8:])

    down(last, z)
    for (a, count), (b, half) in list(zip(offs[:-1], offs[1:]))[::-1]:
        def down_one(t, a=a, b=b):
            p = zp[b + t]
            down(a + 2 * t, swap(p))
            down(a + 2 * t + 1, p)

        if half > 8:
            def down_body(i, carry, down_one=down_one):
                for w in range(4):
                    down_one(i * 4 + w)
                return carry

            lax.fori_loop(0, half // 4, down_body, 0)
        else:
            for t in range(half):
                down_one(t)

    load_o.wait()
    load_t.wait()
    for c in gathers[1:] + rim_copies[1] + rim_copies[2]:
        c.wait_recv()
    for c in halos + gathers + rim_copies[0] + rim_copies[1] + rim_copies[2]:
        c.wait_send()

    def split_body(i, carry):
        for w in range(4):
            e = i * 4 + w
            xs[e] = stacked(ext[:, e].reshape(n_vec * 8, 128))
        return carry

    lax.fori_loop(0, (leaves + 2 * W) // 4, split_body, 0)
    base = li * leaves - W
    slots = tiles.shape[1]
    piece = tiles.shape[2]

    def place(leaf, n):
        return jnp.clip(cols_ref[n, leaf] - base, 0, leaves + 2 * W - 1)

    def near_group(g):
        outs = []
        for w in range(n_vec):
            leaf = g * n_vec + w
            x = jnp.concatenate([xs[place(leaf, n)] for n in range(slots)], axis=1)
            t = jnp.concatenate([stacked(tiles[leaf, n]) for n in range(slots)], axis=1)
            r = lax.dot_general(x, t, NT, preferred_element_type=f32)
            half = r.shape[0] // 2
            r = r[:half] + r[half:]
            outs.append(r[:, :piece] + r[:, piece:])
        nout[:, g] = jnp.concatenate(outs, axis=1).reshape(n_vec, 8, n_vec * piece)

    def near_body(i, carry):
        for w in range(2):
            near_group(i * 2 + w)
        return carry

    half_groups = leaves // n_vec // 2

    def near_copy(d, part):
        u = lax.rem(vi + d, n_vec)
        span = pl.ds(part * half_groups, half_groups)
        return pltpu.make_async_remote_copy(
            src_ref=nout.at[u, span],
            dst_ref=near_ref.at[vi, span],
            send_sem=near_send.at[part, d],
            recv_sem=near_recv.at[part, n_vec - d],
            device_id=(li, u),
            device_id_type=MESH,
        )

    nears = []
    for part in range(2):
        lax.fori_loop(part * half_groups // 2, (part + 1) * half_groups // 2, near_body, 0)
        batch = [near_copy(d, part) for d in (2, 1, 3)]
        for c in batch:
            c.start()
        nears += batch
    keep = pltpu.make_async_copy(nout.at[vi], near_ref.at[vi], near_send.at[0, 0])
    keep.start()

    def far_body(i, carry):
        for w in range(4):
            t = i * 4 + w
            p = zp[t]
            s = swap(p)
            zero = jnp.zeros_like(p)
            for u in range(2):
                pair = 2 * t + u
                first, second = (p, s) if u == 0 else (s, p)
                x = jnp.concatenate(
                    [jnp.where(low, first, zero), jnp.where(low, zero, second)], axis=0
                )
                wt = basis[pl.ds(pl.multiple_of(pair * 128, 128), 128), :]
                r = dot_split(x, wt, NN)
                far_ref[2 * pair] = r[:8]
                far_ref[2 * pair + 1] = r[8:]
        return carry

    lax.fori_loop(0, leaves // 16, far_body, 0)
    keep.wait()
    for c in nears:
        c.wait_recv()
    for c in nears:
        c.wait_send()


def local(
    panels,
    near_tiles,
    near_cols,
    leaf_order,
    leaf_basis,
    local_mats,
    local_flags,
    cross_coupling,
    cross_transfer,
    cross_flags,
):
    rows = panels.shape[0]
    leaves, rank, size = leaf_basis.shape
    n_leaf = lax.axis_size("leaf")
    n_vec = lax.axis_size("vec")
    vmem = pl.BlockSpec(memory_space=pltpu.VMEM)
    hbm = pl.BlockSpec(memory_space=pl.ANY)
    ordered = pl.pallas_call(
        order_kernel,
        out_shape=jax.ShapeDtypeStruct((leaves, rows, size), f32),
        in_specs=[vmem, vmem],
        out_specs=vmem,
        name="order",
    )(panels, leaf_order)
    basis2 = leaf_basis.reshape(leaves * rank, size)
    mats2 = local_mats.reshape(local_mats.shape[1] * rank, 2 * rank)
    groups = leaves // n_vec
    dma = pltpu.SemaphoreType.DMA
    far, near, inverse = pl.pallas_call(
        functools.partial(main_kernel, n_leaf, n_vec),
        out_shape=(
            jax.ShapeDtypeStruct((leaves, rows, size), f32),
            jax.ShapeDtypeStruct((n_vec, groups, rows, size), f32),
            jax.ShapeDtypeStruct((leaves, rows, size), f32),
        ),
        in_specs=[vmem, vmem] + [hbm] * 8,
        out_specs=(vmem, vmem, vmem),
        scratch_shapes=[
            pltpu.SMEM(near_cols.shape[::-1], jnp.int32),
            pltpu.SMEM(local_flags.shape, jnp.int32),
            pltpu.SMEM(cross_flags.shape, jnp.int32),
            pltpu.VMEM(cross_coupling.shape, f32),
            pltpu.VMEM(cross_transfer.shape, f32),
            pltpu.VMEM(near_tiles.shape, f32),
            pltpu.VMEM(basis2.shape, f32),
            pltpu.VMEM(mats2.shape, f32),
            pltpu.VMEM((n_vec, leaves + 2 * W, rows, size), f32),
            pltpu.VMEM((leaves + 2 * W, 2 * n_vec * rows, size), bf16),
            pltpu.VMEM((leaves // 2, rows, size), f32),
            pltpu.VMEM((leaves // 2, rows, size), f32),
            pltpu.VMEM((n_leaf, rows, 2 * rank), f32),
            pltpu.VMEM((n_leaf, rows, 2 * rank), f32),
            pltpu.VMEM((n_vec, groups, rows, size), f32),
            dma((9,)),
            dma((n_vec,)),
            dma((n_vec,)),
            dma((2, n_vec)),
            dma((2, n_vec)),
            dma((n_leaf,)),
            dma((n_leaf,)),
            dma((2, n_vec)),
            dma((2, n_vec)),
        ],
        compiler_params=pltpu.CompilerParams(
            collective_id=0, has_side_effects=True, vmem_limit_bytes=61 * 1024 * 1024
        ),
        name="tree",
    )(
        ordered,
        leaf_order,
        near_cols.T,
        local_flags,
        cross_flags,
        cross_coupling,
        cross_transfer,
        near_tiles,
        basis2,
        mats2,
    )
    return pl.pallas_call(
        restore_kernel,
        out_shape=jax.ShapeDtypeStruct(panels.shape, f32),
        in_specs=[vmem, vmem, vmem],
        out_specs=vmem,
        name="restore",
    )(far, near, inverse)


def solution(mesh):
    return jax.shard_map(
        local,
        mesh=mesh,
        in_specs=(
            P("vec", "leaf"),
            P("leaf", None, "vec", None),
            P("leaf", None),
            P("leaf", None),
            P("leaf", None, None),
            P("leaf", None, None, None),
            P("leaf", None),
            P(),
            P(),
            P(),
        ),
        out_specs=P("vec", "leaf"),
        check_vma=False,
    )
```

```python
import functools
import math

import jax
import jax.numpy as jnp
from jax import lax
from jax.experimental import pallas as pl
from jax.experimental.pallas import tpu as pltpu
from jax.sharding import PartitionSpec as P

W = 8
f32 = jnp.float32
bf16 = jnp.bfloat16
root_half = 1.0 / math.sqrt(2.0)
MESH = pl.DeviceIdType.MESH
NN = (((1,), (0,)), ((), ()))
NT = (((1,), (1,)), ((), ()))


def halves(x):
    high = x.astype(bf16).astype(f32)
    return high, x - high


def stacked(x):
    return jnp.concatenate(halves(x), axis=0).astype(bf16)


def dot_split(x, w, dims):
    rows = x.shape[0]
    lhs = stacked(x)
    high = w.astype(bf16)
    low = (w - high.astype(f32)).astype(bf16)
    r = lax.dot_general(lhs, high, dims, preferred_element_type=f32) + lax.dot_general(
        lhs, low, dims, preferred_element_type=f32
    )
    return r[:rows] + r[rows:]


def hot_of(order_row):
    size = order_row.shape[1]
    rows = lax.broadcasted_iota(jnp.int32, (size, size), 0)
    return jnp.where(rows == order_row, 1.0, 0.0).astype(bf16)


def order_kernel(panels_ref, order_ref, out_ref):
    leaves, size = order_ref.shape
    span = 32

    def body(i, carry):
        for u in range(span):
            leaf = i * span + u
            x = panels_ref[:, pl.ds(pl.multiple_of(leaf * size, size), size)]
            spots = jnp.broadcast_to(order_ref[pl.ds(leaf, 1), :], x.shape)
            out_ref[leaf] = jnp.take_along_axis(x, spots, axis=1)
        return carry

    lax.fori_loop(0, leaves // span, body, 0)


def restore_kernel(far_ref, near_ref, inverse_ref, out_ref):
    leaves, _, size = far_ref.shape
    n_vec = near_ref.shape[0]
    piece = size // n_vec
    rows = out_ref.shape[0]
    block = lax.broadcasted_iota(jnp.int32, (rows, size), 1) // piece

    def group(g):
        parts = [near_ref[v, g] for v in range(n_vec)]
        for u in range(n_vec):
            leaf = g * n_vec + u
            near = parts[0] if u == 0 else pltpu.roll(parts[0], (size - u * piece), 1)
            for v in range(1, n_vec):
                shift = ((v - u) * piece) % size
                moved = parts[v] if shift == 0 else pltpu.roll(parts[v], shift, 1)
                near = jnp.where(block == v, moved, near)
            combined = near + far_ref[leaf]
            spots = inverse_ref[leaf].astype(jnp.int32)
            out_ref[:, pl.ds(pl.multiple_of(leaf * size, size), size)] = jnp.take_along_axis(
                combined, spots, axis=1
            )

    def body(i, carry):
        for w in range(8):
            group(i * 8 + w)
        return carry

    lax.fori_loop(0, leaves // n_vec // 8, body, 0)


def main_kernel(
    n_leaf,
    n_vec,
    own_ref,
    order_ref,
    cols_hbm,
    flags_hbm,
    cross_flags_hbm,
    cross_c_hbm,
    cross_e_hbm,
    tiles_hbm,
    basis_hbm,
    mats_hbm,
    far_ref,
    near_ref,
    inverse_ref,
    cols_ref,
    flags_ref,
    cross_flags_ref,
    cross_c_ref,
    cross_e_ref,
    tiles,
    basis,
    mats,
    ext,
    xs,
    hp,
    zp,
    pay,
    hx,
    nout,
    load_sem,
    gs_send,
    gs_recv,
    halo_send,
    halo_recv,
    pay_send,
    pay_recv,
    near_send,
    near_recv,
):
    leaves = own_ref.shape[0]
    rank = 64
    li = lax.axis_index("leaf")
    vi = lax.axis_index("vec")
    load_b = pltpu.make_async_copy(basis_hbm, basis, load_sem.at[0])
    load_m = pltpu.make_async_copy(mats_hbm, mats, load_sem.at[1])
    load_t = pltpu.make_async_copy(tiles_hbm, tiles, load_sem.at[2])
    load_o = pltpu.make_async_copy(own_ref, ext.at[vi, pl.ds(W, leaves)], load_sem.at[3])
    load_b.start()
    load_m.start()
    load_t.start()
    load_o.start()
    small = [
        pltpu.make_async_copy(src, dst, load_sem.at[4 + i])
        for i, (src, dst) in enumerate(
            [
                (cols_hbm, cols_ref),
                (flags_hbm, flags_ref),
                (cross_flags_hbm, cross_flags_ref),
                (cross_c_hbm, cross_c_ref),
                (cross_e_hbm, cross_e_ref),
            ]
        )
    ]
    for c in small:
        c.start()

    right = lax.rem(li + 1, n_leaf)
    left = lax.rem(li + n_leaf - 1, n_leaf)
    barrier = pltpu.get_barrier_semaphore()
    greeted = 0
    for d in range(1, n_vec):
        pl.semaphore_signal(
            barrier, inc=1, device_id=(li, lax.rem(vi + d, n_vec)), device_id_type=MESH
        )
        greeted += 1
    for d in range(1, n_leaf):
        pl.semaphore_signal(
            barrier, inc=1, device_id=(lax.rem(li + d, n_leaf), vi), device_id_type=MESH
        )
        greeted += 1
    pl.semaphore_wait(barrier, greeted)

    beside = vi + 1 - 2 * lax.rem(vi, 2)
    across = lax.rem(vi + 2, n_vec)

    def gather_copy(kind):
        block = ext.at[across if kind == 2 else vi, pl.ds(W, leaves)]
        return pltpu.make_async_remote_copy(
            src_ref=block if kind == 2 else own_ref,
            dst_ref=block,
            send_sem=gs_send.at[kind],
            recv_sem=gs_recv.at[kind],
            device_id=(li, across if kind == 0 else beside),
            device_id_type=MESH,
        )

    rims = (0, leaves + W)

    def halo_copy(side):
        return pltpu.make_async_remote_copy(
            src_ref=own_ref.at[pl.ds(leaves - W if side == 0 else 0, W)],
            dst_ref=ext.at[vi, pl.ds(rims[side], W)],
            send_sem=halo_send.at[side, 3],
            recv_sem=halo_recv.at[side, 3],
            device_id=(right if side == 0 else left, vi),
            device_id_type=MESH,
        )

    def rim_copy(side, kind):
        block = ext.at[across if kind == 2 else vi, pl.ds(rims[side], W)]
        return pltpu.make_async_remote_copy(
            src_ref=block,
            dst_ref=block,
            send_sem=halo_send.at[side, kind],
            recv_sem=halo_recv.at[side, kind],
            device_id=(li, across if kind == 0 else beside),
            device_id_type=MESH,
        )

    assert n_vec == 4
    gathers = [gather_copy(kind) for kind in range(3)]
    halos = [halo_copy(side) for side in range(2)]
    rim_copies = [[rim_copy(side, kind) for side in range(2)] for kind in range(3)]
    for c in halos + gathers[:2]:
        c.start()

    lane = lax.broadcasted_iota(jnp.int32, (8, 2 * rank), 1)
    low = lane < rank

    def swap(x):
        return pltpu.roll(x, rank, 1)

    load_b.wait()

    def skel_body(i, carry):
        for w in range(8):
            t = i * 8 + w
            sums = []
            for u in range(2):
                pair = t * 2 + u
                x = own_ref[pl.ds(pair * 2, 2)].reshape(16, 128)
                wt = basis[pl.ds(pl.multiple_of(pair * 128, 128), 128), :]
                r = dot_split(x, wt, NT)
                sums.append((r[:8], r[8:]))
            even = sums[0][0] + swap(sums[0][1])
            odd = swap(sums[1][0]) + sums[1][1]
            hp[t] = jnp.where(low, even, odd) * root_half
        return carry

    lax.fori_loop(0, leaves // 32, skel_body, 0)
    for c in halos:
        c.wait_recv()
    for c in rim_copies[0] + rim_copies[1]:
        c.start()
    load_m.wait()

    def mat_pair(q):
        return mats[pl.ds(pl.multiple_of(q * 128, 128), 128), :]

    def up(off, nxt, t):
        r0 = dot_split(hp[off + 2 * t], mat_pair(off + 2 * t), NN)
        r1 = dot_split(hp[off + 2 * t + 1], mat_pair(off + 2 * t + 1), NN)
        hp[nxt + t] = jnp.where(low, swap(r0), r1) * root_half

    pairs = leaves // 4
    offs = []
    off = 0
    while pairs >= 1:
        offs.append((off, pairs))
        off += pairs
        pairs //= 2
    for (a, count), (b, half) in zip(offs[:-1], offs[1:]):
        if half > 8:
            def up_body(i, carry, a=a, b=b):
                for w in range(4):
                    up(a, b, i * 4 + w)
                return carry

            lax.fori_loop(0, half // 4, up_body, 0)
        else:
            for t in range(half):
                up(a, b, t)
    last = offs[-1][0]
    r = dot_split(hp[last], mat_pair(last), NN)
    skel = swap(r) * root_half
    top = mats[pl.ds((last + 1) * 128, rank), :]
    lift = dot_split(skel[:, :rank], top, NN)
    pay[li] = jnp.where(low, skel, lift)

    def pay_copy(d):
        return pltpu.make_async_remote_copy(
            src_ref=pay.at[li],
            dst_ref=pay.at[li],
            send_sem=pay_send.at[d],
            recv_sem=pay_recv.at[n_leaf - d],
            device_id=(lax.rem(li + d, n_leaf), vi),
            device_id_type=MESH,
        )

    pays = [pay_copy(d) for d in range(1, n_leaf)]
    for c in pays:
        c.start()

    counts = lax.broadcasted_iota(jnp.int32, (8, 128), 1).astype(f32).astype(bf16)

    def inverse_body(i, carry):
        for w in range(16):
            leaf = i * 16 + w
            hot = hot_of(order_ref[pl.ds(leaf, 1), :])
            inverse_ref[leaf] = lax.dot_general(counts, hot, NT, preferred_element_type=f32)
        return carry

    lax.fori_loop(0, leaves // 16, inverse_body, 0)
    for c in rim_copies[0]:
        c.wait_recv()
    for c in rim_copies[2]:
        c.start()
    gathers[0].wait_recv()
    gathers[2].start()
    for c in small:
        c.wait()
    for c in pays:
        c.wait_recv()
    for c in pays:
        c.wait_send()

    depth = n_leaf.bit_length() - 1

    def cross_at(c):
        return n_leaf - (n_leaf >> (c - 1))

    lifts = [pay[j] for j in range(n_leaf)]
    at = 0
    starts = {}
    for c in range(1, depth):
        nodes = [
            (lifts[2 * j] + lifts[2 * j + 1]) * root_half for j in range(len(lifts) // 2)
        ]
        nodes = [swap(x) if c == 1 else x for x in nodes]
        starts[c] = at
        for j, x in enumerate(nodes):
            hx[at + j] = x
        at += len(nodes)
        if c < depth - 1:
            lifts = []
            for j, x in enumerate(nodes):
                y = dot_split(x[:, :rank], cross_e_ref[cross_at(c) + j], NN)
                lifts.append(jnp.concatenate([y, y], axis=1))
    z = None
    for c in range(depth - 1, 0, -1):
        node = li >> c
        sibling = node + 1 - 2 * lax.rem(node, 2)
        spot = cross_at(c) + node
        a = cross_flags_ref[spot].astype(f32)
        g = dot_split(a * hx[starts[c] + sibling][:, :rank], cross_c_ref[spot], NT)
        z = g if z is None else g + dot_split(z, cross_e_ref[spot], NT)
    sibling = li + 1 - 2 * lax.rem(li, 2)
    a = flags_ref[0, 2 * (last + 1)].astype(f32)
    x = jnp.where(low, a * pay[sibling], jnp.concatenate([z, z], axis=1))
    z = dot_split(x, top, NT)
    z = jnp.concatenate([z, z], axis=1)

    def down(q, parent):
        h = hp[q]
        a0 = flags_ref[0, 2 * q].astype(f32)
        a1 = flags_ref[0, 2 * q + 1].astype(f32)
        x0 = jnp.where(low, a0 * swap(h), parent)
        x1 = jnp.where(low, a1 * h, parent)
        r = dot_split(jnp.concatenate([x0, x1], axis=0), mat_pair(q), NT)
        zp[q] = jnp.where(low, r[:8], r[8:])

    down(last, z)
    for (a, count), (b, half) in list(zip(offs[:-1], offs[1:]))[::-1]:
        def down_one(t, a=a, b=b):
            p = zp[b + t]
            down(a + 2 * t, swap(p))
            down(a + 2 * t + 1, p)

        if half > 8:
            def down_body(i, carry, down_one=down_one):
                for w in range(4):
                    down_one(i * 4 + w)
                return carry

            lax.fori_loop(0, half // 4, down_body, 0)
        else:
            for t in range(half):
                down_one(t)

    load_o.wait()
    load_t.wait()
    for c in gathers[1:] + rim_copies[1] + rim_copies[2]:
        c.wait_recv()
    for c in halos + gathers + rim_copies[0] + rim_copies[1] + rim_copies[2]:
        c.wait_send()

    def split_body(i, carry):
        for w in range(4):
            e = i * 4 + w
            xs[e] = stacked(ext[:, e].reshape(n_vec * 8, 128))
        return carry

    lax.fori_loop(0, (leaves + 2 * W) // 4, split_body, 0)
    base = li * leaves - W
    slots = tiles.shape[1]
    piece = tiles.shape[2]

    def place(leaf, n):
        return jnp.clip(cols_ref[n, leaf] - base, 0, leaves + 2 * W - 1)

    def near_group(g):
        outs = []
        for w in range(n_vec):
            leaf = g * n_vec + w
            x = jnp.concatenate([xs[place(leaf, n)] for n in range(slots)], axis=1)
            t = jnp.concatenate([stacked(tiles[leaf, n]) for n in range(slots)], axis=1)
            r = lax.dot_general(x, t, NT, preferred_element_type=f32)
            half = r.shape[0] // 2
            r = r[:half] + r[half:]
            outs.append(r[:, :piece] + r[:, piece:])
        nout[:, g] = jnp.concatenate(outs, axis=1).reshape(n_vec, 8, n_vec * piece)

    def near_body(i, carry):
        for w in range(4):
            near_group(i * 4 + w)
        return carry

    half_groups = leaves // n_vec // 2

    def near_copy(d, part):
        u = lax.rem(vi + d, n_vec)
        span = pl.ds(part * half_groups, half_groups)
        return pltpu.make_async_remote_copy(
            src_ref=nout.at[u, span],
            dst_ref=near_ref.at[vi, span],
            send_sem=near_send.at[part, d],
            recv_sem=near_recv.at[part, n_vec - d],
            device_id=(li, u),
            device_id_type=MESH,
        )

    nears = []
    for part in range(2):
        lax.fori_loop(part * half_groups // 4, (part + 1) * half_groups // 4, near_body, 0)
        batch = [near_copy(d, part) for d in (2, 1, 3)]
        for c in batch:
            c.start()
        nears += batch
    keep = pltpu.make_async_copy(nout.at[vi], near_ref.at[vi], near_send.at[0, 0])
    keep.start()

    def far_body(i, carry):
        for w in range(8):
            t = i * 8 + w
            p = zp[t]
            s = swap(p)
            zero = jnp.zeros_like(p)
            for u in range(2):
                pair = 2 * t + u
                first, second = (p, s) if u == 0 else (s, p)
                x = jnp.concatenate(
                    [jnp.where(low, first, zero), jnp.where(low, zero, second)], axis=0
                )
                wt = basis[pl.ds(pl.multiple_of(pair * 128, 128), 128), :]
                r = dot_split(x, wt, NN)
                far_ref[2 * pair] = r[:8]
                far_ref[2 * pair + 1] = r[8:]
        return carry

    lax.fori_loop(0, leaves // 32, far_body, 0)
    keep.wait()
    for c in nears:
        c.wait_recv()
    for c in nears:
        c.wait_send()


def local(
    panels,
    near_tiles,
    near_cols,
    leaf_order,
    leaf_basis,
    local_mats,
    local_flags,
    cross_coupling,
    cross_transfer,
    cross_flags,
):
    rows = panels.shape[0]
    leaves, rank, size = leaf_basis.shape
    n_leaf = lax.axis_size("leaf")
    n_vec = lax.axis_size("vec")
    vmem = pl.BlockSpec(memory_space=pltpu.VMEM)
    hbm = pl.BlockSpec(memory_space=pl.ANY)
    ordered = pl.pallas_call(
        order_kernel,
        out_shape=jax.ShapeDtypeStruct((leaves, rows, size), f32),
        in_specs=[vmem, vmem],
        out_specs=vmem,
        name="order",
    )(panels, leaf_order)
    basis2 = leaf_basis.reshape(leaves * rank, size)
    mats2 = local_mats.reshape(local_mats.shape[1] * rank, 2 * rank)
    groups = leaves // n_vec
    dma = pltpu.SemaphoreType.DMA
    far, near, inverse = pl.pallas_call(
        functools.partial(main_kernel, n_leaf, n_vec),
        out_shape=(
            jax.ShapeDtypeStruct((leaves, rows, size), f32),
            jax.ShapeDtypeStruct((n_vec, groups, rows, size), f32),
            jax.ShapeDtypeStruct((leaves, rows, size), f32),
        ),
        in_specs=[vmem, vmem] + [hbm] * 8,
        out_specs=(vmem, vmem, vmem),
        scratch_shapes=[
            pltpu.SMEM(near_cols.shape[::-1], jnp.int32),
            pltpu.SMEM(local_flags.shape, jnp.int32),
            pltpu.SMEM(cross_flags.shape, jnp.int32),
            pltpu.VMEM(cross_coupling.shape, f32),
            pltpu.VMEM(cross_transfer.shape, f32),
            pltpu.VMEM(near_tiles.shape, f32),
            pltpu.VMEM(basis2.shape, f32),
            pltpu.VMEM(mats2.shape, f32),
            pltpu.VMEM((n_vec, leaves + 2 * W, rows, size), f32),
            pltpu.VMEM((leaves + 2 * W, 2 * n_vec * rows, size), bf16),
            pltpu.VMEM((leaves // 2, rows, size), f32),
            pltpu.VMEM((leaves // 2, rows, size), f32),
            pltpu.VMEM((n_leaf, rows, 2 * rank), f32),
            pltpu.VMEM((n_leaf, rows, 2 * rank), f32),
            pltpu.VMEM((n_vec, groups, rows, size), f32),
            dma((9,)),
            dma((n_vec,)),
            dma((n_vec,)),
            dma((2, n_vec)),
            dma((2, n_vec)),
            dma((n_leaf,)),
            dma((n_leaf,)),
            dma((2, n_vec)),
            dma((2, n_vec)),
        ],
        compiler_params=pltpu.CompilerParams(
            collective_id=0, has_side_effects=True, vmem_limit_bytes=61 * 1024 * 1024
        ),
        name="tree",
    )(
        ordered,
        leaf_order,
        near_cols.T,
        local_flags,
        cross_flags,
        cross_coupling,
        cross_transfer,
        near_tiles,
        basis2,
        mats2,
    )
    return pl.pallas_call(
        restore_kernel,
        out_shape=jax.ShapeDtypeStruct(panels.shape, f32),
        in_specs=[vmem, vmem, vmem],
        out_specs=vmem,
        name="restore",
    )(far, near, inverse)


def solution(mesh):
    return jax.shard_map(
        local,
        mesh=mesh,
        in_specs=(
            P("vec", "leaf"),
            P("leaf", None, "vec", None),
            P("leaf", None),
            P("leaf", None),
            P("leaf", None, None),
            P("leaf", None, None, None),
            P("leaf", None),
            P(),
            P(),
            P(),
        ),
        out_specs=P("vec", "leaf"),
        check_vma=False,
    )
```
